32 devices in a mesh: gx: 8 (over z, x), gy: 4 (over y, core).
Axes of the slice: x: 2, y: 2, z: 4, core: 2. Of those that a mesh axis runs over, the one named last changes fastest.
Arguments:
- mean_field: float32 [16, 128, 1024], P(None, 'gx', 'gy'), may hold values from -6 to 6
- mode_fields: float32 [16, 16, 128, 1024], P(None, None, 'gx', 'gy'), may hold values from -6 to 6
- velocity_east: float32 [16, 128, 1024], P(None, 'gx', 'gy'), may hold values from -6 to 6
- velocity_north: float32 [16, 128, 1024], P(None, 'gx', 'gy'), may hold values from -6 to 6
- flag_east: int32 [16, 128, 1024], P(None, 'gx', 'gy'), may hold values 0 or 1
- flag_north: int32 [16, 128, 1024], P(None, 'gx', 'gy'), may hold values 0 or 1
- ocean_mask: int32 [16, 128, 1024], P(None, 'gx', 'gy'), may hold values 0 or 1
Outputs:
- mean_next: float32 [16, 128, 1024], P(None, 'gx', 'gy')
- modes_next: float32 [16, 16, 128, 1024], P(None, None, 'gx', 'gy')
- factor: float32 [16, 16], replicated
The draws below stay inside these ranges and needn't reach their ends.
Inputs may be any that keep to these rules, and one draw needn't show every extreme that they name: `flag_east`: 1 takes the five-point upwind value biased to the cell of lower index beside the face, 0 the one biased to the higher. `flag_north`: as for the first dimension. `ocean_mask`: 1 marks ocean, 0 land.
All inputs are finite; a program needn't handle non-finite values. No bound on the sum of `flag_east` or of `flag_north` or of `ocean_mask` on one device may be relied on, other than what follows from the above.
Results may differ from the reference program's by a relative error of at most 0.0003.
Values sent between devices are 32-bit elements; how exact they have to be, the bound alone decides.
A program may use at most 128 MiB of HBM per device.

```python
import jax
import jax.numpy as jnp
from jax import lax

M = 16
NZ = 16
NX = 128
NY = 1024


def with_ends(values, stream_key, low, high):
    spot = [jax.random.randint(jax.random.fold_in(stream_key, axis), (), 0, length) for axis, length in enumerate(values.shape)]
    main_axis = values.shape.index(max(values.shape))
    next_to = spot[:main_axis] + [(spot[main_axis] + 1) % values.shape[main_axis]] + spot[main_axis + 1:]
    return values.at[tuple(spot)].set(low).at[tuple(next_to)].set(high)


def block_scale(rng, shape, cuts, least, top_value):
    loudness = 1.0
    for position, parts in cuts:
        heights = jax.random.uniform(jax.random.fold_in(jax.random.fold_in(rng, 6), position), (parts,), jnp.float32, least / len(cuts), top_value / len(cuts))
        loudness = loudness * jnp.repeat(jnp.exp(heights), shape[position] // parts).reshape((-1,) + (1,) * (len(shape) - 1 - position))
    return loudness


def scatter_about(rng, dims, width, bound, cuts=(), held_as=jnp.bfloat16):
    result = width * jax.random.normal(rng, dims, jnp.float32)
    if cuts:
        result = result * block_scale(rng, dims, cuts, -0.22, 0.18)
    return jnp.clip(result, -bound, bound).astype(held_as)


def setup_inputs(seed: int = 0) -> dict:
    key_of = jax.random.split(jax.random.key(seed), 8)
    return {
        "mean_field": scatter_about(key_of[0], (NZ, NX, NY), 1.0, 6.0, ((1, 8), (2, 4)), jnp.float32),
        "mode_fields": scatter_about(key_of[1], (M, NZ, NX, NY), 1.0, 6.0, ((2, 8), (3, 4)), jnp.float32),
        "velocity_east": scatter_about(key_of[2], (NZ, NX, NY), 1.0, 6.0, ((1, 8), (2, 4)), jnp.float32),
        "velocity_north": scatter_about(key_of[3], (NZ, NX, NY), 1.0, 6.0, ((1, 8), (2, 4)), jnp.float32),
        "flag_east": with_ends((jax.random.randint(key_of[4], (NZ, NX, NY), 0, 2) < 1).astype(jnp.int32), jax.random.fold_in(key_of[4], 1), 0, 1),
        "flag_north": with_ends((jax.random.randint(key_of[5], (NZ, NX, NY), 0, 2) < 1).astype(jnp.int32), jax.random.fold_in(key_of[5], 1), 0, 1),
        "ocean_mask": with_ends((jax.random.randint(key_of[6], (NZ, NX, NY), 0, 10) < 9).astype(jnp.int32), jax.random.fold_in(key_of[6], 1), 0, 1),
    }


time_step = 0.1
horiz_diff = 0.05
vert_diff = 0.2

def cells_at(values, axis_dim, first_face, face_count, offset):
    start_index = first_face + offset + 3
    return lax.slice_in_dim(values, start_index, start_index + face_count, axis=axis_dim)

def face_fluxes(values, openness, pos_speed, neg_speed, axis_dim, first_face, face_count):
    centre = cells_at(values, axis_dim, first_face, face_count, 0)
    upper_one = cells_at(values, axis_dim, first_face, face_count, 1)
    lower_one = cells_at(values, axis_dim, first_face, face_count, -1)
    upper_two = cells_at(values, axis_dim, first_face, face_count, 2)
    left_side = (2.0 * cells_at(values, axis_dim, first_face, face_count, -2) - 13.0 * lower_one + 47.0 * centre + 27.0 * upper_one - 3.0 * upper_two) / 60.0
    right_side = (2.0 * cells_at(values, axis_dim, first_face, face_count, 3) - 13.0 * upper_two + 47.0 * upper_one + 27.0 * centre - 3.0 * lower_one) / 60.0
    return openness * (pos_speed * left_side + neg_speed * right_side - horiz_diff * (upper_one - centre))

def direction_fluxes(channels, pos_speed, neg_speed, axis_dim, first_face, face_count):
    mask_part = channels[-1]
    field_part = channels[:-1]
    openness = cells_at(mask_part, axis_dim - 1, first_face, face_count, 0) * cells_at(mask_part, axis_dim - 1, first_face, face_count, 1)
    return face_fluxes(field_part, openness, pos_speed, neg_speed, axis_dim, first_face, face_count)

def lower_inverse(lower_factor):
    order_size = lower_factor.shape[0]
    identity = jnp.eye(order_size, dtype=lower_factor.dtype)
    rows_out = []
    for row_index in range(order_size):
        partial_value = identity[row_index]
        for col_index in range(row_index):
            partial_value = partial_value - lower_factor[row_index, col_index] * rows_out[col_index]
        rows_out.append(partial_value / lower_factor[row_index, row_index])
    return jnp.stack(rows_out)

def reference(mean_field, mode_fields, velocity_east, velocity_north, flag_east, flag_north, ocean_mask):
    fields = jnp.concatenate([mean_field[None], mode_fields], axis=0)
    wet_cells = ocean_mask.astype(jnp.float32)
    east_flag = flag_east.astype(jnp.float32)
    north_flag = flag_north.astype(jnp.float32)
    pos_east = velocity_east * east_flag
    neg_east = velocity_east * (1.0 - east_flag)
    pos_north = velocity_north * north_flag
    neg_north = velocity_north * (1.0 - north_flag)
    levels = fields.shape[1]
    size_x = fields.shape[2]
    size_y = fields.shape[3]

    def level_tendency(level_index):
        fields_here = lax.dynamic_index_in_dim(fields, level_index, 1, keepdims=False)
        level_above = lax.dynamic_index_in_dim(fields, jnp.minimum(level_index + 1, levels - 1), 1, keepdims=False)
        level_below = lax.dynamic_index_in_dim(fields, jnp.maximum(level_index - 1, 0), 1, keepdims=False)
        planes = [lax.dynamic_index_in_dim(plane, level_index, 0, keepdims=False) for plane in (wet_cells, pos_east, neg_east, pos_north, neg_north)]
        stacked = jnp.concatenate([fields_here] + [plane[None] for plane in planes], axis=0)
        padded = jnp.pad(stacked, ((0, 0), (3, 3), (3, 3)))
        across_x = padded[:, :, 3:-3]
        flux_east = direction_fluxes(across_x[:-4], cells_at(across_x[-4], 0, -1, size_x + 1, 0), cells_at(across_x[-3], 0, -1, size_x + 1, 0), 1, -1, size_x + 1)
        tend_x = flux_east[:, :-1] - flux_east[:, 1:]
        across_y = padded[:, 3:-3, :]
        flux_north = direction_fluxes(across_y[:-4], cells_at(across_y[-2], 1, -1, size_y + 1, 0), cells_at(across_y[-1], 1, -1, size_y + 1, 0), 2, -1, size_y + 1)
        tend_y = flux_north[:, :, :-1] - flux_north[:, :, 1:]
        up_flux = jnp.where(level_index < levels - 1, vert_diff * (level_above - fields_here), 0.0)
        down_flux = jnp.where(level_index > 0, vert_diff * (fields_here - level_below), 0.0)
        return planes[0] * (tend_x + tend_y + (up_flux - down_flux))
    per_level = lax.map(level_tendency, jnp.arange(levels, dtype=jnp.int32))
    tendency = jnp.moveaxis(per_level, 0, 1)
    mean_next = mean_field + time_step * tendency[0]
    mode_count = mode_fields.shape[0]
    flat_modes = mode_fields.reshape(mode_count, -1)
    flat_tend = tendency[1:].reshape(mode_count, -1)
    cell_count = float(flat_modes.shape[1])
    highest = lax.Precision.HIGHEST
    projection = jnp.dot(flat_modes, flat_tend.T, precision=highest) / cell_count
    growth = flat_tend - jnp.dot(projection.T, flat_modes, precision=highest)
    updated = flat_modes + time_step * growth
    gram_matrix = jnp.dot(updated, updated.T, precision=highest) / cell_count
    lower_factor = jnp.linalg.cholesky(gram_matrix)
    inverse = lower_inverse(lower_factor)
    modes_next = jnp.dot(inverse, updated, precision=highest).reshape(mode_fields.shape)
    return (mean_next, modes_next, lower_factor.T)
```

```python
import functools

import jax
import jax.numpy as jnp
from jax import lax
from jax.experimental import pallas as pl
from jax.experimental.pallas import tpu as pltpu
from jax.sharding import PartitionSpec as P

time_step = 0.1
horiz_diff = 0.05
vert_diff = 0.2
HALO = 3
LANES = 128
SUB = 8
HIGHEST = lax.Precision.HIGHEST
MESH = pl.DeviceIdType.MESH


def pack_kernel(modes, mean, north, flag, mask, x_last, x_first, y_last, y_first):
    count, _, size_x, size_y = modes.shape
    lane = lax.broadcasted_iota(jnp.int32, (size_x, LANES), 1)
    mask_value = mask[0].astype(jnp.float32)

    def put(packed, tile, source_lane, target_lane, width):
        moved = pltpu.roll(tile, (target_lane - source_lane) % LANES, 1)
        return jnp.where((lane >= target_lane) & (lane < target_lane + width), moved, packed)

    last = jnp.zeros((size_x, LANES), jnp.float32)
    first = jnp.zeros((size_x, LANES), jnp.float32)
    for f in range(count):
        x_last[0, HALO * f : HALO * (f + 1), :] = modes[f, 0, size_x - HALO :, :]
        x_first[0, HALO * f : HALO * (f + 1), :] = modes[f, 0, :HALO, :]
        last = put(last, modes[f, 0, :, size_y - LANES :], LANES - HALO, HALO * f, HALO)
        first = put(first, modes[f, 0, :, :LANES], 0, HALO * f, HALO)
    base = HALO * count
    last = put(last, mean[0, :, size_y - LANES :], LANES - HALO, base, HALO)
    first = put(first, mean[0, :, :LANES], 0, base, HALO)
    base += HALO
    last = put(last, mask_value[:, size_y - LANES :], LANES - 1, base, 1)
    first = put(first, mask_value[:, :LANES], 0, base, 1)
    last = put(last, north[0, :, size_y - LANES :], LANES - 1, base + 1, 1)
    last = put(last, flag[0, :, size_y - LANES :].astype(jnp.float32), LANES - 1, base + 2, 1)
    y_last[0] = last
    y_first[0] = first


def interior_kernel(field, before, after, *rest):
    coefs_x, coefs_y, centre, vertical, out = rest[:6], rest[6:12], rest[12], rest[13], rest[14]
    f = pl.program_id(0)
    levels, size_x, size_y = field.shape[1:]

    def level(k, carry):
        c = field[0, k]
        up = field[0, jnp.minimum(k + 1, levels - 1)]
        down = field[0, jnp.maximum(k - 1, 0)]
        total = centre[k] * c + vertical[k] * (up + down)
        shifts = (-3, -2, -1, 1, 2, 3)
        for i, s in enumerate(shifts):
            total += coefs_x[i][k] * pltpu.roll(c, (-s) % size_x, 0)
        left = pltpu.roll(before[k], LANES - HALO - HALO * f, 1)
        right = pltpu.roll(after[k], LANES - HALO * f, 1)
        wide = jnp.concatenate([left, c, right], axis=1)
        for i, s in enumerate(shifts):
            moved = pltpu.roll(wide, (-s) % (size_y + 2 * LANES), 1)
            total += coefs_y[i][k] * moved[:, LANES : LANES + size_y]
        out[0, k] = total
        return carry

    lax.fori_loop(0, levels, level, 0)


def gram_kernel(modes, partial, low, high, l3, l2, l1, h1, h2, h3, tend, gram, low_rows, high_rows, same, cross):
    z = pl.program_id(0)
    count, _, size_x, size_y = modes.shape
    rows = low.shape[1]

    @pl.when(z == 0)
    def _():
        low_rows[...] = jnp.zeros_like(low_rows)
        high_rows[...] = jnp.zeros_like(high_rows)
        same[...] = jnp.zeros_like(same)
        cross[...] = jnp.zeros_like(cross)

    low_rows[SUB : SUB + rows, :] = low[0]
    high_rows[SUB : SUB + rows, :] = high[0]
    for f in range(count):
        at = SUB + HALO * f
        tend[f, 0] = partial[f, 0]
        tend[f, 0, :SUB, :] = partial[f, 0, :SUB, :] + (
            l3[0] * low_rows[at : at + SUB, :]
            + l2[0] * low_rows[at + 1 : at + 1 + SUB, :]
            + l1[0] * low_rows[at + 2 : at + 2 + SUB, :]
        )
        tend[f, 0, size_x - SUB :, :] = tend[f, 0, size_x - SUB :, :] + (
            h1[0] * high_rows[at - 7 : at - 7 + SUB, :]
            + h2[0] * high_rows[at - 6 : at - 6 + SUB, :]
            + h3[0] * high_rows[at - 5 : at - 5 + SUB, :]
        )
    contract = (((1,), (1,)), ((), ()))
    for part in range(size_x // SUB):
        cut = slice(part * SUB, (part + 1) * SUB)
        both = jnp.concatenate(
            [modes[:, 0, cut, :].reshape(count * SUB, size_y), tend[:, 0, cut, :].reshape(count * SUB, size_y)], axis=0
        )
        coarse = both.astype(jnp.bfloat16)
        fine = (both - coarse.astype(jnp.float32)).astype(jnp.bfloat16)
        same[...] += lax.dot_general(coarse, coarse, contract, preferred_element_type=jnp.float32)
        cross[...] += lax.dot_general(coarse, fine, contract, preferred_element_type=jnp.float32)

    @pl.when(z == pl.num_programs(0) - 1)
    def _():
        wide = 2 * count * SUB
        row = lax.broadcasted_iota(jnp.int32, (wide, wide), 0)
        col = lax.broadcasted_iota(jnp.int32, (wide, wide), 1)
        kept = (row % SUB) == (col % SUB)
        total = jnp.where(kept, same[...] + cross[...] + cross[...].T, 0.0)
        pick = (
            lax.broadcasted_iota(jnp.int32, (2 * count, wide), 1) // SUB
            == lax.broadcasted_iota(jnp.int32, (2 * count, wide), 0)
        ).astype(jnp.float32)
        half = jnp.dot(pick, total, precision=HIGHEST, preferred_element_type=jnp.float32)
        gram[...] = lax.dot_general(half, pick, contract, precision=HIGHEST, preferred_element_type=jnp.float32)


def reduce_kernel(nx, ny, cells, count, part, factor, mix, gathered, send_sem, recv_sem):
    gx, gy = lax.axis_index("gx"), lax.axis_index("gy")
    me = gx * ny + gy
    devices = nx * ny

    def place(k):
        other = lax.rem(me + k, devices)
        return other, (other // ny, lax.rem(other, ny))

    barrier = pltpu.get_barrier_semaphore()

    def greet(k, carry):
        _, where = place(k)
        pl.semaphore_signal(barrier, inc=1, device_id=where, device_id_type=MESH)
        return carry

    lax.fori_loop(1, devices, greet, 0)
    gathered[me] = part[...]
    pl.semaphore_wait(barrier, devices - 1)

    def out_copy(k):
        _, where = place(k)
        return pltpu.make_async_remote_copy(
            src_ref=part,
            dst_ref=gathered.at[me],
            send_sem=send_sem.at[k],
            recv_sem=recv_sem.at[me],
            device_id=where,
            device_id_type=MESH,
        )

    def in_copy(k):
        other, where = place(k)
        return pltpu.make_async_remote_copy(
            src_ref=part,
            dst_ref=gathered.at[other],
            send_sem=send_sem.at[k],
            recv_sem=recv_sem.at[other],
            device_id=where,
            device_id_type=MESH,
        )

    def send(k, carry):
        out_copy(k).start()
        return carry

    def arrive(k, carry):
        in_copy(k).wait_recv()
        return carry

    def sent(k, carry):
        out_copy(k).wait_send()
        return carry

    lax.fori_loop(1, devices, send, 0)
    lax.fori_loop(1, devices, arrive, 0)
    lax.fori_loop(1, devices, sent, 0)

    def add(k, total):
        return total + gathered[k]

    total = lax.fori_loop(1, devices, add, gathered[0]) / cells
    two = 2 * count
    row = lax.broadcasted_iota(jnp.int32, (count, two), 0)
    col = lax.broadcasted_iota(jnp.int32, (count, two), 1)
    contract = (((1,), (1,)), ((), ()))
    update = jnp.where(
        col < count,
        jnp.where(col == row, 1.0, 0.0) - time_step * total[count:, :],
        jnp.where(col == row + count, time_step, 0.0),
    )
    padding = jnp.zeros((count, two), jnp.float32)
    halfway = jnp.dot(update, total, precision=HIGHEST, preferred_element_type=jnp.float32)
    work = lax.dot_general(
        halfway,
        jnp.concatenate([update, padding], axis=0),
        contract,
        precision=HIGHEST,
        preferred_element_type=jnp.float32,
    )
    work = work + jnp.where(col == row + count, 1.0, 0.0)
    for j in range(count):
        pivot_row = work[j : j + 1, :] * lax.rsqrt(work[j : j + 1, j : j + 1])
        column = work[:, j : j + 1] * lax.rsqrt(work[j : j + 1, j : j + 1])
        work = jnp.where(row > j, work - column * pivot_row, jnp.where(row == j, pivot_row, work))
    factor[...] = jnp.where(col[:, :count] >= row[:, :count], work[:, :count], 0.0)
    inverse = jnp.where(col >= count, work, 0.0)
    mix[...] = jnp.dot(
        inverse,
        jnp.concatenate([padding, update], axis=0),
        precision=HIGHEST,
        preferred_element_type=jnp.float32,
    )


def combine_kernel(mix, modes, tend, out, weights, weights_fine):
    z = pl.program_id(0)
    count, _, size_x, size_y = modes.shape

    @pl.when(z == 0)
    def _():
        tall, wide = count * SUB, 2 * count * SUB
        spread = (
            lax.broadcasted_iota(jnp.int32, (tall, count), 0) // SUB
            == lax.broadcasted_iota(jnp.int32, (tall, count), 1)
        ).astype(jnp.float32)
        along = (
            lax.broadcasted_iota(jnp.int32, (2 * count, wide), 1) // SUB
            == lax.broadcasted_iota(jnp.int32, (2 * count, wide), 0)
        ).astype(jnp.float32)
        whole = jnp.dot(
            jnp.dot(spread, mix[...], precision=HIGHEST, preferred_element_type=jnp.float32),
            along,
            precision=HIGHEST,
            preferred_element_type=jnp.float32,
        )
        row = lax.broadcasted_iota(jnp.int32, (tall, wide), 0)
        col = lax.broadcasted_iota(jnp.int32, (tall, wide), 1)
        whole = jnp.where((row % SUB) == (col % SUB), whole, 0.0)
        coarse = whole.astype(jnp.bfloat16)
        weights[...] = coarse
        weights_fine[...] = (whole - coarse.astype(jnp.float32)).astype(jnp.bfloat16)

    for part in range(size_x // SUB):
        cut = slice(part * SUB, (part + 1) * SUB)
        both = jnp.concatenate(
            [modes[:, 0, cut, :].reshape(count * SUB, size_y), tend[:, 0, cut, :].reshape(count * SUB, size_y)], axis=0
        )
        coarse = both.astype(jnp.bfloat16)
        fine = (both - coarse.astype(jnp.float32)).astype(jnp.bfloat16)
        result = (
            jnp.dot(weights[...], fine, preferred_element_type=jnp.float32)
            + jnp.dot(weights_fine[...], coarse, preferred_element_type=jnp.float32)
            + jnp.dot(weights[...], coarse, preferred_element_type=jnp.float32)
        )
        out[:, 0, cut, :] = result.reshape(count, SUB, size_y)


def stencil(pos, neg, openness, cells, axis):
    face = {
        -2: openness * (2.0 * pos) / 60.0,
        -1: openness * (-13.0 * pos - 3.0 * neg) / 60.0,
        0: openness * ((47.0 * pos + 27.0 * neg) / 60.0 + horiz_diff),
        1: openness * ((27.0 * pos + 47.0 * neg) / 60.0 - horiz_diff),
        2: openness * (-3.0 * pos - 13.0 * neg) / 60.0,
        3: openness * (2.0 * neg) / 60.0,
    }
    size = cells.shape[axis]
    result = {}
    for s in range(-3, 4):
        value = 0.0
        if s + 1 in face:
            value = value + lax.slice_in_dim(face[s + 1], 0, size, axis=axis)
        if s in face:
            value = value - lax.slice_in_dim(face[s], 1, size + 1, axis=axis)
        result[s] = cells * value
    return result


def shards(mean_field, mode_fields, velocity_east, velocity_north, flag_east, flag_north, ocean_mask):
    count, levels, size_x, size_y = mode_fields.shape
    nx, ny = lax.axis_size("gx"), lax.axis_size("gy")
    f32 = jnp.float32

    def up(value, axis):
        return lax.ppermute(value, axis, [(i, i + 1) for i in range(lax.axis_size(axis) - 1)])

    def down(value, axis):
        return lax.ppermute(value, axis, [(i + 1, i) for i in range(lax.axis_size(axis) - 1)])

    wet = ocean_mask.astype(f32)
    east = flag_east.astype(f32)
    north = flag_north.astype(f32)

    aux_last = jnp.concatenate(
        [mean_field[:, -HALO:], wet[:, -1:], velocity_east[:, -1:], east[:, -1:]], axis=1
    ).transpose(1, 0, 2)
    aux_first = jnp.concatenate([mean_field[:, :HALO], wet[:, :1]], axis=1).transpose(1, 0, 2)

    modes_level = pl.BlockSpec((count, 1, size_x, size_y), lambda z: (0, z, 0, 0))
    plane = pl.BlockSpec((1, size_x, size_y), lambda z: (z, 0, 0))
    layers = pl.BlockSpec((1, HALO * count, size_y), lambda z: (z, 0, 0))
    columns = pl.BlockSpec((1, size_x, LANES), lambda z: (z, 0, 0))
    x_last, x_first, y_last, y_first = pl.pallas_call(
        pack_kernel,
        grid=(levels,),
        in_specs=[modes_level, plane, plane, plane, plane],
        out_specs=[layers, layers, columns, columns],
        out_shape=[jax.ShapeDtypeStruct((levels, HALO * count, size_y), f32)] * 2
        + [jax.ShapeDtypeStruct((levels, size_x, LANES), f32)] * 2,
    )(mode_fields, mean_field, velocity_north, flag_north, ocean_mask)

    y_before, y_after = up(y_last, "gy"), down(y_first, "gy")
    aux_before = up(aux_last, "gx").transpose(1, 0, 2)
    aux_after = down(aux_first, "gx").transpose(1, 0, 2)
    x_before, x_after = up(x_last, "gx"), down(x_first, "gx")

    speed = jnp.concatenate([aux_before[:, 4:5], velocity_east], axis=1)
    side = jnp.concatenate([aux_before[:, 5:6], east], axis=1)
    cells = jnp.concatenate([aux_before[:, 3:4], wet, aux_after[:, 3:4]], axis=1)
    dx = stencil(speed * side, speed * (1.0 - side), cells[:, :-1] * cells[:, 1:], wet, 1)
    at = HALO * count
    speed = jnp.concatenate([y_before[:, :, at + 4 : at + 5], velocity_north], axis=2)
    side = jnp.concatenate([y_before[:, :, at + 5 : at + 6], north], axis=2)
    cells = jnp.concatenate([y_before[:, :, at + 3 : at + 4], wet, y_after[:, :, at + 3 : at + 4]], axis=2)
    dy = stencil(speed * side, speed * (1.0 - side), cells[:, :, :-1] * cells[:, :, 1:], wet, 2)
    centre = dx[0] + dy[0] - 2.0 * vert_diff * wet
    vertical = vert_diff * wet

    shifts = (-3, -2, -1, 1, 2, 3)
    spot = lax.broadcasted_iota(jnp.int32, (levels, size_x, size_y), 1)
    inner = [jnp.where((spot + s >= 0) & (spot + s < size_x), dx[s], 0.0) for s in shifts]
    outer = [
        jnp.where(spot + s < 0, dx[s], 0.0)[:, :SUB] if s < 0 else jnp.where(spot + s >= size_x, dx[s], 0.0)[:, -SUB:]
        for s in shifts
    ]

    mean_x = jnp.concatenate([aux_before[:, :HALO], mean_field, aux_after[:, :HALO]], axis=1)
    mean_y = jnp.concatenate([y_before[:, :, at : at + HALO], mean_field, y_after[:, :, at : at + HALO]], axis=2)
    above = jnp.concatenate([mean_field[1:], mean_field[-1:]], axis=0)
    below = jnp.concatenate([mean_field[:1], mean_field[:-1]], axis=0)
    mean_tend = centre * mean_field + vertical * (above + below)
    for s in shifts:
        mean_tend = mean_tend + dx[s] * lax.slice_in_dim(mean_x, HALO + s, HALO + s + size_x, axis=1)
        mean_tend = mean_tend + dy[s] * lax.slice_in_dim(mean_y, HALO + s, HALO + s + size_y, axis=2)
    mean_next = mean_field + time_step * mean_tend

    one_field = pl.BlockSpec((1, levels, size_x, size_y), lambda f: (f, 0, 0, 0))
    grid_whole = pl.BlockSpec((levels, size_x, size_y), lambda f: (0, 0, 0))
    halo_whole = pl.BlockSpec((levels, size_x, LANES), lambda f: (0, 0, 0))
    cost = pl.CostEstimate(flops=60 * mode_fields.size, bytes_accessed=12 * mode_fields.size, transcendentals=0)
    partial = pl.pallas_call(
        interior_kernel,
        grid=(count,),
        in_specs=[one_field, halo_whole, halo_whole] + [grid_whole] * 14,
        out_specs=one_field,
        out_shape=jax.ShapeDtypeStruct(mode_fields.shape, f32),
        cost_estimate=cost,
    )(mode_fields, y_before, y_after, *inner, *[dy[s] for s in shifts], centre, vertical)

    edge = pl.BlockSpec((1, SUB, size_y), lambda z: (z, 0, 0))
    gram_whole = pl.BlockSpec((2 * count, 2 * count), lambda z: (0, 0))
    wide = 2 * count * SUB
    tend, gram = pl.pallas_call(
        gram_kernel,
        grid=(levels,),
        in_specs=[modes_level, modes_level, layers, layers] + [edge] * 6,
        out_specs=[modes_level, gram_whole],
        out_shape=[jax.ShapeDtypeStruct(mode_fields.shape, f32), jax.ShapeDtypeStruct((2 * count, 2 * count), f32)],
        scratch_shapes=[pltpu.VMEM((HALO * count + 2 * SUB, size_y), f32)] * 2 + [pltpu.VMEM((wide, wide), f32)] * 2,
    )(mode_fields, partial, x_before, x_after, *outer)

    cell_count = float(levels * size_x * size_y * nx * ny)
    vmem = pl.BlockSpec(memory_space=pltpu.VMEM)
    factor, mix = pl.pallas_call(
        functools.partial(reduce_kernel, nx, ny, cell_count, count),
        in_specs=[vmem],
        out_specs=[vmem, vmem],
        out_shape=[jax.ShapeDtypeStruct((count, count), f32), jax.ShapeDtypeStruct((count, 2 * count), f32)],
        scratch_shapes=[
            pltpu.VMEM((nx * ny, 2 * count, 2 * count), f32),
            pltpu.SemaphoreType.DMA((nx * ny,)),
            pltpu.SemaphoreType.DMA((nx * ny,)),
        ],
        compiler_params=pltpu.CompilerParams(collective_id=0, has_side_effects=True),
    )(gram)

    modes_next = pl.pallas_call(
        combine_kernel,
        grid=(levels,),
        in_specs=[pl.BlockSpec((count, 2 * count), lambda z: (0, 0)), modes_level, modes_level],
        out_specs=modes_level,
        out_shape=jax.ShapeDtypeStruct(mode_fields.shape, f32),
        scratch_shapes=[pltpu.VMEM((count * SUB, wide), jnp.bfloat16)] * 2,
    )(mix, mode_fields, tend)
    return (mean_next, modes_next, factor)


def solution(mesh):
    grid = P(None, "gx", "gy")
    return jax.shard_map(
        shards,
        mesh=mesh,
        in_specs=(grid, P(None, None, "gx", "gy"), grid, grid, grid, grid, grid),
        out_specs=(grid, P(None, None, "gx", "gy"), P()),
        check_vma=False,
    )
```

```python
import functools

import jax
import jax.numpy as jnp
from jax import lax
from jax.experimental import pallas as pl
from jax.experimental.pallas import tpu as pltpu
from jax.sharding import PartitionSpec as P

time_step = 0.1
horiz_diff = 0.05
vert_diff = 0.2
HALO = 3
LANES = 128
SUB = 8
HIGHEST = lax.Precision.HIGHEST
MESH = pl.DeviceIdType.MESH


def pack_kernel(modes, mean, north, flag, mask, x_last, x_first, y_last, y_first):
    count, levels, size_x, size_y = modes.shape
    lane = lax.broadcasted_iota(jnp.int32, (size_x, LANES), 1)

    def put(packed, tile, source_lane, target_lane, width):
        moved = pltpu.roll(tile, (target_lane - source_lane) % LANES, 1)
        return jnp.where((lane >= target_lane) & (lane < target_lane + width), moved, packed)

    for k in range(levels):
        mask_value = mask[k].astype(jnp.float32)
        last = jnp.zeros((size_x, LANES), jnp.float32)
        first = jnp.zeros((size_x, LANES), jnp.float32)
        for f in range(count):
            x_last[k, HALO * f : HALO * (f + 1), :] = modes[f, k, size_x - HALO :, :]
            x_first[k, HALO * f : HALO * (f + 1), :] = modes[f, k, :HALO, :]
            last = put(last, modes[f, k, :, size_y - LANES :], LANES - HALO, HALO * f, HALO)
            first = put(first, modes[f, k, :, :LANES], 0, HALO * f, HALO)
        base = HALO * count
        last = put(last, mean[k, :, size_y - LANES :], LANES - HALO, base, HALO)
        first = put(first, mean[k, :, :LANES], 0, base, HALO)
        base += HALO
        last = put(last, mask_value[:, size_y - LANES :], LANES - 1, base, 1)
        first = put(first, mask_value[:, :LANES], 0, base, 1)
        last = put(last, north[k, :, size_y - LANES :], LANES - 1, base + 1, 1)
        last = put(last, flag[k, :, size_y - LANES :].astype(jnp.float32), LANES - 1, base + 2, 1)
        y_last[k] = last
        y_first[k] = first


def interior_kernel(field, before, after, *rest):
    coefs_x, coefs_y, centre, vertical, out = rest[:6], rest[6:12], rest[12], rest[13], rest[14]
    group, levels, size_x, size_y = field.shape
    f0 = pl.program_id(0) * group
    lane = lax.broadcasted_iota(jnp.int32, (size_x, LANES), 1)
    tiles = size_y // LANES
    shifts = (-3, -2, -1, 1, 2, 3)

    def level(k, carry):
        above = jnp.minimum(k + 1, levels - 1)
        below = jnp.maximum(k - 1, 0)
        for g in range(group):
            f = f0 + g
            left = pltpu.roll(before[k], LANES - HALO - HALO * f, 1)
            right = pltpu.roll(after[k], LANES - HALO * f, 1)
            row = [left] + [field[g, k, :, t * LANES : (t + 1) * LANES] for t in range(tiles)] + [right]
            for t in range(tiles):
                cut = slice(t * LANES, (t + 1) * LANES)
                c = row[t + 1]
                total = centre[k, :, cut] * c + vertical[k, :, cut] * (field[g, above, :, cut] + field[g, below, :, cut])
                for i, s in enumerate(shifts):
                    total += coefs_x[i][k, :, cut] * pltpu.roll(c, (-s) % size_x, 0)
                    if s < 0:
                        mixed = jnp.where(lane >= LANES + s, row[t], c)
                    else:
                        mixed = jnp.where(lane < s, row[t + 2], c)
                    total += coefs_y[i][k, :, cut] * pltpu.roll(mixed, (-s) % LANES, 1)
                out[g, k, :, cut] = total
        return carry

    lax.fori_loop(0, levels, level, 0, unroll=2)


def gram_kernel(modes, partial, low, high, l3, l2, l1, h1, h2, h3, tend, gram, low_rows, high_rows, total):
    z = pl.program_id(0)
    count, levels, size_x, size_y = modes.shape
    rows = low.shape[1]
    wide = 2 * count * SUB

    @pl.when(z == 0)
    def _():
        low_rows[...] = jnp.zeros_like(low_rows)
        high_rows[...] = jnp.zeros_like(high_rows)
        total[...] = jnp.zeros_like(total)

    for k in range(levels):
        low_rows[k, SUB : SUB + rows, :] = low[k]
        high_rows[k, SUB : SUB + rows, :] = high[k]
        for f in range(count):
            at = SUB + HALO * f
            if size_x > 2 * SUB:
                tend[f, k] = partial[f, k]
            tend[f, k, :SUB, :] = partial[f, k, :SUB, :] + (
                l3[k] * low_rows[k, at : at + SUB, :]
                + l2[k] * low_rows[k, at + 1 : at + 1 + SUB, :]
                + l1[k] * low_rows[k, at + 2 : at + 2 + SUB, :]
            )
            base = tend if size_x == SUB else partial
            tend[f, k, size_x - SUB :, :] = base[f, k, size_x - SUB :, :] + (
                h1[k] * high_rows[k, at - 7 : at - 7 + SUB, :]
                + h2[k] * high_rows[k, at - 6 : at - 6 + SUB, :]
                + h3[k] * high_rows[k, at - 5 : at - 5 + SUB, :]
            )
    contract = (((1,), (1,)), ((), ()))
    for part in range(size_x // SUB):
        cut = slice(part * SUB, (part + 1) * SUB)
        both = jnp.concatenate(
            [
                jnp.concatenate([ref[:, k, cut, :].reshape(count * SUB, size_y) for k in range(levels)], axis=1)
                for ref in (modes, tend)
            ],
            axis=0,
        )
        coarse = both.astype(jnp.bfloat16)
        fine = (both - coarse.astype(jnp.float32)).astype(jnp.bfloat16)
        total[...] += lax.dot_general(
            jnp.concatenate([coarse, fine], axis=0), coarse, contract, preferred_element_type=jnp.float32
        )

    @pl.when(z == pl.num_programs(0) - 1)
    def _():
        row = lax.broadcasted_iota(jnp.int32, (wide, wide), 0)
        col = lax.broadcasted_iota(jnp.int32, (wide, wide), 1)
        kept = (row % SUB) == (col % SUB)
        cross = total[wide:, :]
        summed = jnp.where(kept, total[:wide, :] + cross + cross.T, 0.0)
        pick = (
            lax.broadcasted_iota(jnp.int32, (2 * count, wide), 1) // SUB
            == lax.broadcasted_iota(jnp.int32, (2 * count, wide), 0)
        ).astype(jnp.float32)
        width = gram.shape[1]
        spread = (
            lax.broadcasted_iota(jnp.int32, (wide, width), 0) // SUB
            == lax.broadcasted_iota(jnp.int32, (wide, width), 1) % (2 * count)
        ).astype(jnp.float32)
        half = jnp.dot(pick, summed, precision=HIGHEST, preferred_element_type=jnp.float32)
        full = jnp.dot(half, spread, precision=HIGHEST, preferred_element_type=jnp.float32)
        height = gram.shape[0]
        block = lax.broadcasted_iota(jnp.int32, gram.shape, 1) // (2 * count)
        packed = full[:height]
        for b in range(1, 2 * count // height):
            packed = jnp.where(block == b, full[b * height : (b + 1) * height], packed)
        gram[...] = packed


def reduce_kernel(nx, ny, part, total, gathered, send_sem, recv_sem):
    gx, gy = lax.axis_index("gx"), lax.axis_index("gy")
    me = gx * ny + gy
    devices = nx * ny

    def place(k):
        other = lax.rem(me + k, devices)
        return other, (other // ny, lax.rem(other, ny))

    barrier = pltpu.get_barrier_semaphore()

    def greet(k, carry):
        _, where = place(k)
        pl.semaphore_signal(barrier, inc=1, device_id=where, device_id_type=MESH)
        return carry

    lax.fori_loop(1, devices, greet, 0)
    gathered[me] = part[...]
    pl.semaphore_wait(barrier, devices - 1)

    def out_copy(k):
        _, where = place(k)
        return pltpu.make_async_remote_copy(
            src_ref=part,
            dst_ref=gathered.at[me],
            send_sem=send_sem.at[k],
            recv_sem=recv_sem.at[me],
            device_id=where,
            device_id_type=MESH,
        )

    def in_copy(k):
        other, where = place(k)
        return pltpu.make_async_remote_copy(
            src_ref=part,
            dst_ref=gathered.at[other],
            send_sem=send_sem.at[k],
            recv_sem=recv_sem.at[other],
            device_id=where,
            device_id_type=MESH,
        )

    def send(k, carry):
        out_copy(k).start()
        return carry

    def arrive(k, carry):
        in_copy(k).wait_recv()
        return carry

    def sent(k, carry):
        out_copy(k).wait_send()
        return carry

    lax.fori_loop(1, devices, send, 0)
    lax.fori_loop(1, devices, arrive, 0)
    lax.fori_loop(1, devices, sent, 0)

    def add(k, value):
        return value + gathered[k]

    total[...] = lax.fori_loop(1, devices, add, gathered[0])


def solve(packed, count, cells):
    two = 2 * count
    height, width = packed.shape
    block = lax.broadcasted_iota(jnp.int32, packed.shape, 1) // two
    stacked = jnp.concatenate([jnp.where(block == b, packed, 0.0) for b in range(two // height)], axis=0)
    fold = (
        lax.broadcasted_iota(jnp.int32, (width, two), 0) % two == lax.broadcasted_iota(jnp.int32, (width, two), 1)
    ).astype(jnp.float32)
    total = jnp.dot(stacked, fold, precision=HIGHEST, preferred_element_type=jnp.float32) / cells
    row = lax.broadcasted_iota(jnp.int32, (count, two), 0)
    col = lax.broadcasted_iota(jnp.int32, (count, two), 1)
    contract = (((1,), (1,)), ((), ()))
    update = jnp.where(
        col < count,
        jnp.where(col == row, 1.0, 0.0) - time_step * total[count:, :],
        jnp.where(col == row + count, time_step, 0.0),
    )
    padding = jnp.zeros((count, two), jnp.float32)
    halfway = jnp.dot(update, total, precision=HIGHEST, preferred_element_type=jnp.float32)
    work = lax.dot_general(
        halfway,
        jnp.concatenate([update, padding], axis=0),
        contract,
        precision=HIGHEST,
        preferred_element_type=jnp.float32,
    )
    work = work + jnp.where(col == row + count, 1.0, 0.0)
    for j in range(count):
        column = jnp.broadcast_to(work[:, j : j + 1], (count, two))
        scale = lax.rsqrt(column[j : j + 1, :])
        pivot_row = work[j : j + 1, :] * scale
        work = jnp.where(row > j, work - (column * scale) * pivot_row, jnp.where(row == j, pivot_row, work))
    factor = jnp.where(col >= row, work, 0.0)[:, :count]
    inverse = jnp.where(col >= count, work, 0.0)
    mix = jnp.dot(
        inverse,
        jnp.concatenate([padding, update], axis=0),
        precision=HIGHEST,
        preferred_element_type=jnp.float32,
    )
    return factor, mix


def combine_kernel(cells, packed, modes, tend, out, factor, weights):
    z = pl.program_id(0)
    count, levels, size_x, size_y = modes.shape
    tall, wide = count * SUB, 2 * count * SUB

    @pl.when(z == 0)
    def _():
        factor[...], mix = solve(packed[...], count, cells)
        spread = (
            lax.broadcasted_iota(jnp.int32, (tall, count), 0) // SUB
            == lax.broadcasted_iota(jnp.int32, (tall, count), 1)
        ).astype(jnp.float32)
        along = (
            lax.broadcasted_iota(jnp.int32, (2 * count, wide), 1) // SUB
            == lax.broadcasted_iota(jnp.int32, (2 * count, wide), 0)
        ).astype(jnp.float32)
        whole = jnp.dot(
            jnp.dot(spread, mix, precision=HIGHEST, preferred_element_type=jnp.float32),
            along,
            precision=HIGHEST,
            preferred_element_type=jnp.float32,
        )
        row = lax.broadcasted_iota(jnp.int32, (tall, wide), 0)
        col = lax.broadcasted_iota(jnp.int32, (tall, wide), 1)
        whole = jnp.where((row % SUB) == (col % SUB), whole, 0.0)
        coarse = whole.astype(jnp.bfloat16)
        weights[:tall, :] = coarse
        weights[tall:, :] = (whole - coarse.astype(jnp.float32)).astype(jnp.bfloat16)

    for k in range(levels):
        for part in range(size_x // SUB):
            cut = slice(part * SUB, (part + 1) * SUB)
            both = jnp.concatenate(
                [modes[:, k, cut, :].reshape(count * SUB, size_y), tend[:, k, cut, :].reshape(count * SUB, size_y)],
                axis=0,
            )
            coarse = both.astype(jnp.bfloat16)
            fine = (both - coarse.astype(jnp.float32)).astype(jnp.bfloat16)
            main = jnp.dot(weights[...], coarse, preferred_element_type=jnp.float32)
            result = main[:tall] + (
                main[tall:] + jnp.dot(weights[:tall, :], fine, preferred_element_type=jnp.float32)
            )
            out[:, k, cut, :] = result.reshape(count, SUB, size_y)


def divisor(size, most):
    return max(d for d in range(1, most + 1) if size % d == 0)


def stencil(pos, neg, openness, cells, axis):
    face = {
        -2: openness * (2.0 * pos) / 60.0,
        -1: openness * (-13.0 * pos - 3.0 * neg) / 60.0,
        0: openness * ((47.0 * pos + 27.0 * neg) / 60.0 + horiz_diff),
        1: openness * ((27.0 * pos + 47.0 * neg) / 60.0 - horiz_diff),
        2: openness * (-3.0 * pos - 13.0 * neg) / 60.0,
        3: openness * (2.0 * neg) / 60.0,
    }
    size = cells.shape[axis]
    result = {}
    for s in range(-3, 4):
        value = 0.0
        if s + 1 in face:
            value = value + lax.slice_in_dim(face[s + 1], 0, size, axis=axis)
        if s in face:
            value = value - lax.slice_in_dim(face[s], 1, size + 1, axis=axis)
        result[s] = cells * value
    return result


def shards(mean_field, mode_fields, velocity_east, velocity_north, flag_east, flag_north, ocean_mask):
    count, levels, size_x, size_y = mode_fields.shape
    nx, ny = lax.axis_size("gx"), lax.axis_size("gy")
    f32 = jnp.float32

    def up(value, axis):
        return lax.ppermute(value, axis, [(i, i + 1) for i in range(lax.axis_size(axis) - 1)])

    def down(value, axis):
        return lax.ppermute(value, axis, [(i + 1, i) for i in range(lax.axis_size(axis) - 1)])

    wet = ocean_mask.astype(f32)
    east = flag_east.astype(f32)
    north = flag_north.astype(f32)

    aux_last = jnp.concatenate(
        [mean_field[:, -HALO:], wet[:, -1:], velocity_east[:, -1:], east[:, -1:]], axis=1
    ).transpose(1, 0, 2)
    aux_first = jnp.concatenate([mean_field[:, :HALO], wet[:, :1]], axis=1).transpose(1, 0, 2)

    step = divisor(levels, 4)
    modes_level = pl.BlockSpec((count, step, size_x, size_y), lambda z: (0, z, 0, 0))
    plane = pl.BlockSpec((step, size_x, size_y), lambda z: (z, 0, 0))
    layers = pl.BlockSpec((step, HALO * count, size_y), lambda z: (z, 0, 0))
    columns = pl.BlockSpec((step, size_x, LANES), lambda z: (z, 0, 0))
    x_last, x_first, y_last, y_first = pl.pallas_call(
        pack_kernel,
        grid=(levels // step,),
        in_specs=[modes_level, plane, plane, plane, plane],
        out_specs=[layers, layers, columns, columns],
        out_shape=[jax.ShapeDtypeStruct((levels, HALO * count, size_y), f32)] * 2
        + [jax.ShapeDtypeStruct((levels, size_x, LANES), f32)] * 2,
    )(mode_fields, mean_field, velocity_north, flag_north, ocean_mask)

    y_before, y_after = up(y_last, "gy"), down(y_first, "gy")
    aux_before = up(aux_last, "gx").transpose(1, 0, 2)
    aux_after = down(aux_first, "gx").transpose(1, 0, 2)
    x_before, x_after = up(x_last, "gx"), down(x_first, "gx")

    speed = jnp.concatenate([aux_before[:, 4:5], velocity_east], axis=1)
    side = jnp.concatenate([aux_before[:, 5:6], east], axis=1)
    cells = jnp.concatenate([aux_before[:, 3:4], wet, aux_after[:, 3:4]], axis=1)
    dx = stencil(speed * side, speed * (1.0 - side), cells[:, :-1] * cells[:, 1:], wet, 1)
    at = HALO * count
    speed = jnp.concatenate([y_before[:, :, at + 4 : at + 5], velocity_north], axis=2)
    side = jnp.concatenate([y_before[:, :, at + 5 : at + 6], north], axis=2)
    cells = jnp.concatenate([y_before[:, :, at + 3 : at + 4], wet, y_after[:, :, at + 3 : at + 4]], axis=2)
    dy = stencil(speed * side, speed * (1.0 - side), cells[:, :, :-1] * cells[:, :, 1:], wet, 2)
    centre = dx[0] + dy[0] - 2.0 * vert_diff * wet
    vertical = vert_diff * wet

    shifts = (-3, -2, -1, 1, 2, 3)
    spot = lax.broadcasted_iota(jnp.int32, (levels, size_x, size_y), 1)
    inner = [jnp.where((spot + s >= 0) & (spot + s < size_x), dx[s], 0.0) for s in shifts]
    outer = [
        jnp.where(spot + s < 0, dx[s], 0.0)[:, :SUB] if s < 0 else jnp.where(spot + s >= size_x, dx[s], 0.0)[:, -SUB:]
        for s in shifts
    ]

    mean_x = jnp.concatenate([aux_before[:, :HALO], mean_field, aux_after[:, :HALO]], axis=1)
    mean_y = jnp.concatenate([y_before[:, :, at : at + HALO], mean_field, y_after[:, :, at : at + HALO]], axis=2)
    above = jnp.concatenate([mean_field[1:], mean_field[-1:]], axis=0)
    below = jnp.concatenate([mean_field[:1], mean_field[:-1]], axis=0)
    mean_tend = centre * mean_field + vertical * (above + below)
    for s in shifts:
        mean_tend = mean_tend + dx[s] * lax.slice_in_dim(mean_x, HALO + s, HALO + s + size_x, axis=1)
        mean_tend = mean_tend + dy[s] * lax.slice_in_dim(mean_y, HALO + s, HALO + s + size_y, axis=2)
    mean_next = mean_field + time_step * mean_tend

    group = divisor(count, 2)
    one_field = pl.BlockSpec((group, levels, size_x, size_y), lambda f: (f, 0, 0, 0))
    grid_whole = pl.BlockSpec((levels, size_x, size_y), lambda f: (0, 0, 0))
    halo_whole = pl.BlockSpec((levels, size_x, LANES), lambda f: (0, 0, 0))
    cost = pl.CostEstimate(flops=60 * mode_fields.size, bytes_accessed=12 * mode_fields.size, transcendentals=0)
    partial = pl.pallas_call(
        interior_kernel,
        grid=(count // group,),
        in_specs=[one_field, halo_whole, halo_whole] + [grid_whole] * 14,
        out_specs=one_field,
        out_shape=jax.ShapeDtypeStruct(mode_fields.shape, f32),
        cost_estimate=cost,
    )(mode_fields, y_before, y_after, *inner, *[dy[s] for s in shifts], centre, vertical)

    edge = pl.BlockSpec((step, SUB, size_y), lambda z: (z, 0, 0))
    wide = 2 * count * SUB
    packed = (4 * count * count // LANES, LANES)
    tend, gram = pl.pallas_call(
        gram_kernel,
        grid=(levels // step,),
        in_specs=[modes_level, modes_level, layers, layers] + [edge] * 6,
        out_specs=[modes_level, pl.BlockSpec(packed, lambda z: (0, 0))],
        out_shape=[jax.ShapeDtypeStruct(mode_fields.shape, f32), jax.ShapeDtypeStruct(packed, f32)],
        scratch_shapes=[pltpu.VMEM((step, HALO * count + 2 * SUB, size_y), f32)] * 2
        + [pltpu.VMEM((2 * wide, wide), f32)],
    )(mode_fields, partial, x_before, x_after, *outer)

    cell_count = float(levels * size_x * size_y * nx * ny)
    vmem = pl.BlockSpec(memory_space=pltpu.VMEM)
    gram = pl.pallas_call(
        functools.partial(reduce_kernel, nx, ny),
        in_specs=[vmem],
        out_specs=vmem,
        out_shape=jax.ShapeDtypeStruct(packed, f32),
        scratch_shapes=[
            pltpu.VMEM((nx * ny,) + packed, f32),
            pltpu.SemaphoreType.DMA((nx * ny,)),
            pltpu.SemaphoreType.DMA((nx * ny,)),
        ],
        compiler_params=pltpu.CompilerParams(collective_id=0, has_side_effects=True),
    )(gram)

    modes_next, factor = pl.pallas_call(
        functools.partial(combine_kernel, cell_count),
        grid=(levels // step,),
        in_specs=[pl.BlockSpec(packed, lambda z: (0, 0)), modes_level, modes_level],
        out_specs=[modes_level, pl.BlockSpec((count, count), lambda z: (0, 0))],
        out_shape=[jax.ShapeDtypeStruct(mode_fields.shape, f32), jax.ShapeDtypeStruct((count, count), f32)],
        scratch_shapes=[pltpu.VMEM((wide, wide), jnp.bfloat16)],
    )(gram, mode_fields, tend)
    return (mean_next, modes_next, factor)


def solution(mesh):
    grid = P(None, "gx", "gy")
    return jax.shard_map(
        shards,
        mesh=mesh,
        in_specs=(grid, P(None, None, "gx", "gy"), grid, grid, grid, grid, grid),
        out_specs=(grid, P(None, None, "gx", "gy"), P()),
        check_vma=False,
    )
```

```python
import functools

import jax
import jax.numpy as jnp
from jax import lax
from jax.experimental import pallas as pl
from jax.experimental.pallas import tpu as pltpu
from jax.sharding import PartitionSpec as P


time_step = 0.1
horiz_diff = 0.05
vert_diff = 0.2
HALO = 3
LANES = 128
SUB = 8
HIGHEST = lax.Precision.HIGHEST
MESH = pl.DeviceIdType.MESH


def layers_kernel(modes, mean, east, flag, mask, x_last, x_first, aux_last, aux_first):
    count, levels, size_x, _ = modes.shape

    @pl.when(pl.program_id(0) == 0)
    def _():
        for j in range(HALO):
            aux_last[j] = mean[:, size_x - HALO + j, :]
            aux_first[j] = mean[:, j, :]
        aux_last[HALO] = mask[:, size_x - 1, :].astype(jnp.float32)
        aux_first[HALO] = mask[:, 0, :].astype(jnp.float32)
        aux_last[HALO + 1] = east[:, size_x - 1, :]
        aux_last[HALO + 2] = flag[:, size_x - 1, :].astype(jnp.float32)

    for k in range(levels):
        for f in range(count):
            x_last[k, HALO * f : HALO * (f + 1), :] = modes[f, k, size_x - HALO :, :]
            x_first[k, HALO * f : HALO * (f + 1), :] = modes[f, k, :HALO, :]


def columns_kernel(after_layers, modes, mean, north, flag_north, mask, y_last, y_first):
    count, levels, size_x, size_y = modes.shape
    lane = lax.broadcasted_iota(jnp.int32, (size_x, LANES), 1)

    def put(packed, tile, source_lane, target_lane, width):
        moved = pltpu.roll(tile, (target_lane - source_lane) % LANES, 1)
        return jnp.where((lane >= target_lane) & (lane < target_lane + width), moved, packed)

    for k in range(levels):
        mask_value = mask[k].astype(jnp.float32)
        last = jnp.zeros((size_x, LANES), jnp.float32)
        first = jnp.zeros((size_x, LANES), jnp.float32)
        for f in range(count):
            last = put(last, modes[f, k, :, size_y - LANES :], LANES - HALO, HALO * f, HALO)
            first = put(first, modes[f, k, :, :LANES], 0, HALO * f, HALO)
        base = HALO * count
        last = put(last, mean[k, :, size_y - LANES :], LANES - HALO, base, HALO)
        first = put(first, mean[k, :, :LANES], 0, base, HALO)
        base += HALO
        last = put(last, mask_value[:, size_y - LANES :], LANES - 1, base, 1)
        first = put(first, mask_value[:, :LANES], 0, base, 1)
        last = put(last, north[k, :, size_y - LANES :], LANES - 1, base + 1, 1)
        last = put(last, flag_north[k, :, size_y - LANES :].astype(jnp.float32), LANES - 1, base + 2, 1)
        y_last[k] = last
        y_first[k] = first


def interior_kernel(field, before, after, *rest):
    coefs_x, coefs_y, centre, vertical, out = rest[:6], rest[6:12], rest[12], rest[13], rest[14]
    group, levels, size_x, size_y = field.shape
    f0 = pl.program_id(0) * group
    lane = lax.broadcasted_iota(jnp.int32, (size_x, LANES), 1)
    tiles = size_y // LANES
    shifts = (-3, -2, -1, 1, 2, 3)

    def level(k, carry):
        above = jnp.minimum(k + 1, levels - 1)
        below = jnp.maximum(k - 1, 0)
        for g in range(group):
            f = f0 + g
            left = pltpu.roll(before[k], LANES - HALO - HALO * f, 1)
            right = pltpu.roll(after[k], LANES - HALO * f, 1)
            row = [left] + [field[g, k, :, t * LANES : (t + 1) * LANES] for t in range(tiles)] + [right]
            for t in range(tiles):
                cut = slice(t * LANES, (t + 1) * LANES)
                c = row[t + 1]
                total = centre[k, :, cut] * c + vertical[k, :, cut] * (field[g, above, :, cut] + field[g, below, :, cut])
                for i, s in enumerate(shifts):
                    total += coefs_x[i][k, :, cut] * pltpu.roll(c, (-s) % size_x, 0)
                    if s < 0:
                        mixed = jnp.where(lane >= LANES + s, row[t], c)
                    else:
                        mixed = jnp.where(lane < s, row[t + 2], c)
                    total += coefs_y[i][k, :, cut] * pltpu.roll(mixed, (-s) % LANES, 1)
                out[g, k, :, cut] = total
        return carry

    lax.fori_loop(0, levels, level, 0, unroll=2)


def gram_kernel(
    nx, ny, modes, partial, low, high, l3, l2, l1, h1, h2, h3, tend, gram,
    low_rows, high_rows, total, mine, gathered, send_sem, recv_sem,
):
    z = pl.program_id(0)
    me = lax.axis_index("gx") * ny + lax.axis_index("gy")
    devices = nx * ny
    barrier = pltpu.get_barrier_semaphore()
    count, levels, size_x, size_y = modes.shape

    def place(k):
        other = lax.rem(me + k, devices)
        return other, (other // ny, lax.rem(other, ny))

    def copy(k, slot):
        return pltpu.make_async_remote_copy(
            src_ref=mine,
            dst_ref=gathered.at[slot],
            send_sem=send_sem.at[k],
            recv_sem=recv_sem.at[slot],
            device_id=place(k)[1],
            device_id_type=MESH,
        )

    rows = low.shape[1]
    wide = 2 * count * SUB

    @pl.when(z == 0)
    def _():
        def greet(k, carry):
            pl.semaphore_signal(barrier, inc=1, device_id=place(k)[1], device_id_type=MESH)
            return carry

        lax.fori_loop(1, devices, greet, 0)
        low_rows[...] = jnp.zeros_like(low_rows)
        high_rows[...] = jnp.zeros_like(high_rows)
        total[...] = jnp.zeros_like(total)

    for k in range(levels):
        low_rows[k, SUB : SUB + rows, :] = low[k]
        high_rows[k, SUB : SUB + rows, :] = high[k]
        for f in range(count):
            at = SUB + HALO * f
            if size_x > 2 * SUB:
                tend[f, k] = partial[f, k]
            tend[f, k, :SUB, :] = partial[f, k, :SUB, :] + (
                l3[k] * low_rows[k, at : at + SUB, :]
                + l2[k] * low_rows[k, at + 1 : at + 1 + SUB, :]
                + l1[k] * low_rows[k, at + 2 : at + 2 + SUB, :]
            )
            base = tend if size_x == SUB else partial
            tend[f, k, size_x - SUB :, :] = base[f, k, size_x - SUB :, :] + (
                h1[k] * high_rows[k, at - 7 : at - 7 + SUB, :]
                + h2[k] * high_rows[k, at - 6 : at - 6 + SUB, :]
                + h3[k] * high_rows[k, at - 5 : at - 5 + SUB, :]
            )
    contract = (((1,), (1,)), ((), ()))
    for part in range(size_x // SUB):
        cut = slice(part * SUB, (part + 1) * SUB)
        both = jnp.concatenate(
            [
                jnp.concatenate([ref[:, k, cut, :].reshape(count * SUB, size_y) for k in range(levels)], axis=1)
                for ref in (modes, tend)
            ],
            axis=0,
        )
        coarse = both.astype(jnp.bfloat16)
        fine = (both - coarse.astype(jnp.float32)).astype(jnp.bfloat16)
        total[...] += lax.dot_general(
            jnp.concatenate([coarse, fine], axis=0), coarse, contract, preferred_element_type=jnp.float32
        )

    @pl.when(z == pl.num_programs(0) - 1)
    def _():
        row = lax.broadcasted_iota(jnp.int32, (wide, wide), 0)
        col = lax.broadcasted_iota(jnp.int32, (wide, wide), 1)
        kept = (row % SUB) == (col % SUB)
        cross = total[wide:, :]
        summed = jnp.where(kept, total[:wide, :] + cross + cross.T, 0.0)
        pick = (
            lax.broadcasted_iota(jnp.int32, (2 * count, wide), 1) // SUB
            == lax.broadcasted_iota(jnp.int32, (2 * count, wide), 0)
        ).astype(jnp.float32)
        width = gram.shape[1]
        spread = (
            lax.broadcasted_iota(jnp.int32, (wide, width), 0) // SUB
            == lax.broadcasted_iota(jnp.int32, (wide, width), 1) % (2 * count)
        ).astype(jnp.float32)
        half = jnp.dot(pick, summed, precision=HIGHEST, preferred_element_type=jnp.float32)
        full = jnp.dot(half, spread, precision=HIGHEST, preferred_element_type=jnp.float32)
        height = gram.shape[0]
        block = lax.broadcasted_iota(jnp.int32, gram.shape, 1) // (2 * count)
        packed = full[:height]
        for b in range(1, 2 * count // height):
            packed = jnp.where(block == b, full[b * height : (b + 1) * height], packed)
        mine[...] = packed
        gathered[me] = packed
        pl.semaphore_wait(barrier, devices - 1)

        def send(k, carry):
            copy(k, me).start()
            return carry

        def arrive(k, carry):
            copy(k, place(k)[0]).wait_recv()
            return carry

        def sent(k, carry):
            copy(k, me).wait_send()
            return carry

        def add(k, value):
            return value + gathered[k]

        lax.fori_loop(1, devices, send, 0)
        lax.fori_loop(1, devices, arrive, 0)
        gram[...] = lax.fori_loop(1, devices, add, gathered[0])
        lax.fori_loop(1, devices, sent, 0)


def solve(packed, count, cells):
    two = 2 * count
    height, width = packed.shape
    block = lax.broadcasted_iota(jnp.int32, packed.shape, 1) // two
    stacked = jnp.concatenate([jnp.where(block == b, packed, 0.0) for b in range(two // height)], axis=0)
    fold = (
        lax.broadcasted_iota(jnp.int32, (width, two), 0) % two == lax.broadcasted_iota(jnp.int32, (width, two), 1)
    ).astype(jnp.float32)
    total = jnp.dot(stacked, fold, precision=HIGHEST, preferred_element_type=jnp.float32) / cells
    row = lax.broadcasted_iota(jnp.int32, (count, two), 0)
    col = lax.broadcasted_iota(jnp.int32, (count, two), 1)
    contract = (((1,), (1,)), ((), ()))
    update = jnp.where(
        col < count,
        jnp.where(col == row, 1.0, 0.0) - time_step * total[count:, :],
        jnp.where(col == row + count, time_step, 0.0),
    )
    padding = jnp.zeros((count, two), jnp.float32)
    halfway = jnp.dot(update, total, precision=HIGHEST, preferred_element_type=jnp.float32)
    work = lax.dot_general(
        halfway,
        jnp.concatenate([update, padding], axis=0),
        contract,
        precision=HIGHEST,
        preferred_element_type=jnp.float32,
    )
    work = work + jnp.where(col == row + count, 1.0, 0.0)
    for j in range(count):
        column = jnp.broadcast_to(work[:, j : j + 1], (count, two))
        scale = lax.rsqrt(column[j : j + 1, :])
        pivot_row = work[j : j + 1, :] * scale
        work = jnp.where(row > j, work - (column * scale) * pivot_row, jnp.where(row == j, pivot_row, work))
    factor = jnp.where(col >= row, work, 0.0)[:, :count]
    inverse = jnp.where(col >= count, work, 0.0)
    mix = jnp.dot(
        inverse,
        jnp.concatenate([padding, update], axis=0),
        precision=HIGHEST,
        preferred_element_type=jnp.float32,
    )
    return factor, mix


def combine_kernel(cells, packed, modes, tend, out, factor, weights):
    z = pl.program_id(0)
    count, levels, size_x, size_y = modes.shape
    tall, wide = count * SUB, 2 * count * SUB

    @pl.when(z == 0)
    def _():
        factor[...], mix = solve(packed[...], count, cells)
        spread = (
            lax.broadcasted_iota(jnp.int32, (tall, count), 0) // SUB
            == lax.broadcasted_iota(jnp.int32, (tall, count), 1)
        ).astype(jnp.float32)
        along = (
            lax.broadcasted_iota(jnp.int32, (2 * count, wide), 1) // SUB
            == lax.broadcasted_iota(jnp.int32, (2 * count, wide), 0)
        ).astype(jnp.float32)
        whole = jnp.dot(
            jnp.dot(spread, mix, precision=HIGHEST, preferred_element_type=jnp.float32),
            along,
            precision=HIGHEST,
            preferred_element_type=jnp.float32,
        )
        row = lax.broadcasted_iota(jnp.int32, (tall, wide), 0)
        col = lax.broadcasted_iota(jnp.int32, (tall, wide), 1)
        whole = jnp.where((row % SUB) == (col % SUB), whole, 0.0)
        coarse = whole.astype(jnp.bfloat16)
        weights[:tall, :] = coarse
        weights[tall:, :] = (whole - coarse.astype(jnp.float32)).astype(jnp.bfloat16)

    for k in range(levels):
        for part in range(size_x // SUB):
            cut = slice(part * SUB, (part + 1) * SUB)
            both = jnp.concatenate(
                [modes[:, k, cut, :].reshape(count * SUB, size_y), tend[:, k, cut, :].reshape(count * SUB, size_y)],
                axis=0,
            )
            coarse = both.astype(jnp.bfloat16)
            fine = (both - coarse.astype(jnp.float32)).astype(jnp.bfloat16)
            main = jnp.dot(weights[...], coarse, preferred_element_type=jnp.float32)
            result = main[:tall] + (
                main[tall:] + jnp.dot(weights[:tall, :], fine, preferred_element_type=jnp.float32)
            )
            out[:, k, cut, :] = result.reshape(count, SUB, size_y)


def divisor(size, most):
    return max(d for d in range(1, most + 1) if size % d == 0)


def stencil(pos, neg, openness, cells, axis):
    face = {
        -2: openness * (2.0 * pos) / 60.0,
        -1: openness * (-13.0 * pos - 3.0 * neg) / 60.0,
        0: openness * ((47.0 * pos + 27.0 * neg) / 60.0 + horiz_diff),
        1: openness * ((27.0 * pos + 47.0 * neg) / 60.0 - horiz_diff),
        2: openness * (-3.0 * pos - 13.0 * neg) / 60.0,
        3: openness * (2.0 * neg) / 60.0,
    }
    size = cells.shape[axis]
    result = {}
    for s in range(-3, 4):
        value = 0.0
        if s + 1 in face:
            value = value + lax.slice_in_dim(face[s + 1], 0, size, axis=axis)
        if s in face:
            value = value - lax.slice_in_dim(face[s], 1, size + 1, axis=axis)
        result[s] = cells * value
    return result


def section(mean_field, mode_fields, velocity_east, velocity_north, flag_east, flag_north, ocean_mask):
    count, levels, size_x, size_y = mode_fields.shape
    nx, ny = lax.axis_size("gx"), lax.axis_size("gy")
    f32 = jnp.float32

    def up(value, axis):
        return lax.ppermute(value, axis, [(i, i + 1) for i in range(lax.axis_size(axis) - 1)])

    def down(value, axis):
        return lax.ppermute(value, axis, [(i + 1, i) for i in range(lax.axis_size(axis) - 1)])

    wet = ocean_mask.astype(f32)
    east = flag_east.astype(f32)
    north = flag_north.astype(f32)

    step = divisor(levels, 4)
    modes_level = pl.BlockSpec((count, step, size_x, size_y), lambda z: (0, z, 0, 0))
    layers = pl.BlockSpec((step, HALO * count, size_y), lambda z: (z, 0, 0))
    whole_plane = pl.BlockSpec((levels, size_x, size_y), lambda z: (0, 0, 0))
    side_rows = (HALO + 3, HALO + 1)
    x_last, x_first, aux_last, aux_first = pl.pallas_call(
        layers_kernel,
        grid=(levels // step,),
        in_specs=[modes_level] + [whole_plane] * 4,
        out_specs=[layers, layers] + [pl.BlockSpec((n, levels, size_y), lambda z: (0, 0, 0)) for n in side_rows],
        out_shape=[jax.ShapeDtypeStruct((levels, HALO * count, size_y), f32)] * 2
        + [jax.ShapeDtypeStruct((n, levels, size_y), f32) for n in side_rows],
    )(mode_fields, mean_field, velocity_east, flag_east, ocean_mask)
    aux_before = up(aux_last, "gx")
    aux_after = down(aux_first, "gx")
    x_before = up(x_last, "gx")
    x_after = down(x_first, "gx")
    aux_before = aux_before.transpose(1, 0, 2)
    aux_after = aux_after.transpose(1, 0, 2)

    half = SUB if levels % SUB == 0 else levels
    plane = pl.BlockSpec((half, size_x, size_y), lambda z: (z, 0, 0))
    columns = pl.BlockSpec((half, size_x, LANES), lambda z: (z, 0, 0))
    y_last, y_first = pl.pallas_call(
        columns_kernel,
        grid=(levels // half,),
        in_specs=[pl.BlockSpec(memory_space=pl.ANY)]
        + [pl.BlockSpec((count, half, size_x, size_y), lambda z: (0, z, 0, 0))]
        + [plane] * 4,
        out_specs=[columns, columns],
        out_shape=[jax.ShapeDtypeStruct((levels, size_x, LANES), f32)] * 2,
    )(x_last, mode_fields, mean_field, velocity_north, flag_north, ocean_mask)
    y_before, y_after = up(y_last, "gy"), down(y_first, "gy")

    speed = jnp.concatenate([aux_before[:, 4:5], velocity_east], axis=1)
    side = jnp.concatenate([aux_before[:, 5:6], east], axis=1)
    cells = jnp.concatenate([aux_before[:, 3:4], wet, aux_after[:, 3:4]], axis=1)
    dx = stencil(speed * side, speed * (1.0 - side), cells[:, :-1] * cells[:, 1:], wet, 1)
    at = HALO * count
    speed = jnp.concatenate([y_before[:, :, at + 4 : at + 5], velocity_north], axis=2)
    side = jnp.concatenate([y_before[:, :, at + 5 : at + 6], north], axis=2)
    cells = jnp.concatenate([y_before[:, :, at + 3 : at + 4], wet, y_after[:, :, at + 3 : at + 4]], axis=2)
    dy = stencil(speed * side, speed * (1.0 - side), cells[:, :, :-1] * cells[:, :, 1:], wet, 2)
    centre = dx[0] + dy[0] - 2.0 * vert_diff * wet
    vertical = vert_diff * wet

    shifts = (-3, -2, -1, 1, 2, 3)
    spot = lax.broadcasted_iota(jnp.int32, (levels, size_x, size_y), 1)
    inner = [jnp.where((spot + s >= 0) & (spot + s < size_x), dx[s], 0.0) for s in shifts]
    outer = [
        jnp.where(spot + s < 0, dx[s], 0.0)[:, :SUB] if s < 0 else jnp.where(spot + s >= size_x, dx[s], 0.0)[:, -SUB:]
        for s in shifts
    ]

    mean_x = jnp.concatenate([aux_before[:, :HALO], mean_field, aux_after[:, :HALO]], axis=1)
    mean_y = jnp.concatenate([y_before[:, :, at : at + HALO], mean_field, y_after[:, :, at : at + HALO]], axis=2)
    above = jnp.concatenate([mean_field[1:], mean_field[-1:]], axis=0)
    below = jnp.concatenate([mean_field[:1], mean_field[:-1]], axis=0)
    mean_tend = centre * mean_field + vertical * (above + below)
    for s in shifts:
        mean_tend = mean_tend + dx[s] * lax.slice_in_dim(mean_x, HALO + s, HALO + s + size_x, axis=1)
        mean_tend = mean_tend + dy[s] * lax.slice_in_dim(mean_y, HALO + s, HALO + s + size_y, axis=2)
    mean_next = mean_field + time_step * mean_tend

    group = divisor(count, 2)
    one_field = pl.BlockSpec((group, levels, size_x, size_y), lambda f: (f, 0, 0, 0))
    grid_whole = pl.BlockSpec((levels, size_x, size_y), lambda f: (0, 0, 0))
    halo_whole = pl.BlockSpec((levels, size_x, LANES), lambda f: (0, 0, 0))
    cost = pl.CostEstimate(flops=60 * mode_fields.size, bytes_accessed=12 * mode_fields.size, transcendentals=0)
    partial = pl.pallas_call(
        interior_kernel,
        grid=(count // group,),
        in_specs=[one_field, halo_whole, halo_whole] + [grid_whole] * 14,
        out_specs=one_field,
        out_shape=jax.ShapeDtypeStruct(mode_fields.shape, f32),
        cost_estimate=cost,
    )(mode_fields, y_before, y_after, *inner, *[dy[s] for s in shifts], centre, vertical)

    edge = pl.BlockSpec((step, SUB, size_y), lambda z: (z, 0, 0))
    wide = 2 * count * SUB
    packed = (4 * count * count // LANES, LANES)
    tend, gram = pl.pallas_call(
        functools.partial(gram_kernel, nx, ny),
        grid=(levels // step,),
        in_specs=[modes_level, modes_level, layers, layers] + [edge] * 6,
        out_specs=[modes_level, pl.BlockSpec(packed, lambda z: (0, 0))],
        out_shape=[jax.ShapeDtypeStruct(mode_fields.shape, f32), jax.ShapeDtypeStruct(packed, f32)],
        scratch_shapes=[pltpu.VMEM((step, HALO * count + 2 * SUB, size_y), f32)] * 2
        + [
            pltpu.VMEM((2 * wide, wide), f32),
            pltpu.VMEM(packed, f32),
            pltpu.VMEM((nx * ny,) + packed, f32),
            pltpu.SemaphoreType.DMA((nx * ny,)),
            pltpu.SemaphoreType.DMA((nx * ny,)),
        ],
        compiler_params=pltpu.CompilerParams(collective_id=0, has_side_effects=True),
    )(mode_fields, partial, x_before, x_after, *outer)

    cell_count = float(levels * size_x * size_y * nx * ny)
    modes_next, factor = pl.pallas_call(
        functools.partial(combine_kernel, cell_count),
        grid=(levels // step,),
        in_specs=[pl.BlockSpec(packed, lambda z: (0, 0)), modes_level, modes_level],
        out_specs=[modes_level, pl.BlockSpec((count, count), lambda z: (0, 0))],
        out_shape=[jax.ShapeDtypeStruct(mode_fields.shape, f32), jax.ShapeDtypeStruct((count, count), f32)],
        scratch_shapes=[pltpu.VMEM((wide, wide), jnp.bfloat16)],
    )(gram, mode_fields, tend)
    return (mean_next, modes_next, factor)


def solution(mesh):
    grid = P(None, "gx", "gy")
    return jax.shard_map(
        section,
        mesh=mesh,
        in_specs=(grid, P(None, None, "gx", "gy"), grid, grid, grid, grid, grid),
        out_specs=(grid, P(None, None, "gx", "gy"), P()),
        check_vma=False,
    )
```

```python
import functools

import jax
import jax.numpy as jnp
from jax import lax
from jax.experimental import pallas as pl
from jax.experimental.pallas import tpu as pltpu
from jax.sharding import PartitionSpec as P


time_step = 0.1
horiz_diff = 0.05
vert_diff = 0.2
HALO = 3
LANES = 128
SUB = 8
HIGHEST = lax.Precision.HIGHEST
MESH = pl.DeviceIdType.MESH


def layers_kernel(modes, mean, east, flag, mask, x_last, x_first, aux_last, aux_first):
    count, levels, size_x, _ = modes.shape

    @pl.when(pl.program_id(0) == 0)
    def _():
        for j in range(HALO):
            aux_last[j] = mean[:, size_x - HALO + j, :]
            aux_first[j] = mean[:, j, :]
        aux_last[HALO] = mask[:, size_x - 1, :].astype(jnp.float32)
        aux_first[HALO] = mask[:, 0, :].astype(jnp.float32)
        aux_last[HALO + 1] = east[:, size_x - 1, :]
        aux_last[HALO + 2] = flag[:, size_x - 1, :].astype(jnp.float32)

    for k in range(levels):
        for f in range(count):
            x_last[k, HALO * f : HALO * (f + 1), :] = modes[f, k, size_x - HALO :, :]
            x_first[k, HALO * f : HALO * (f + 1), :] = modes[f, k, :HALO, :]


def columns_kernel(after_layers, modes, mean, north, flag_north, mask, y_last, y_first):
    count, levels, size_x, size_y = modes.shape
    lane = lax.broadcasted_iota(jnp.int32, (size_x, LANES), 1)

    def put(packed, tile, source_lane, target_lane, width):
        moved = pltpu.roll(tile, (target_lane - source_lane) % LANES, 1)
        return jnp.where((lane >= target_lane) & (lane < target_lane + width), moved, packed)

    for k in range(levels):
        mask_value = mask[k].astype(jnp.float32)
        last = jnp.zeros((size_x, LANES), jnp.float32)
        first = jnp.zeros((size_x, LANES), jnp.float32)
        for f in range(count):
            last = put(last, modes[f, k, :, size_y - LANES :], LANES - HALO, HALO * f, HALO)
            first = put(first, modes[f, k, :, :LANES], 0, HALO * f, HALO)
        base = HALO * count
        last = put(last, mean[k, :, size_y - LANES :], LANES - HALO, base, HALO)
        first = put(first, mean[k, :, :LANES], 0, base, HALO)
        base += HALO
        last = put(last, mask_value[:, size_y - LANES :], LANES - 1, base, 1)
        first = put(first, mask_value[:, :LANES], 0, base, 1)
        last = put(last, north[k, :, size_y - LANES :], LANES - 1, base + 1, 1)
        last = put(last, flag_north[k, :, size_y - LANES :].astype(jnp.float32), LANES - 1, base + 2, 1)
        y_last[k] = last
        y_first[k] = first


def face_weights(pos, neg, openness):
    return {
        -2: openness * (2.0 * pos) / 60.0,
        -1: openness * (-13.0 * pos - 3.0 * neg) / 60.0,
        0: openness * ((47.0 * pos + 27.0 * neg) / 60.0 + horiz_diff),
        1: openness * ((27.0 * pos + 47.0 * neg) / 60.0 - horiz_diff),
        2: openness * (-3.0 * pos - 13.0 * neg) / 60.0,
        3: openness * (2.0 * neg) / 60.0,
    }


def stencil(speed, side, cells, speed_before, side_before, cells_before, cells_after, axis):
    size = cells.shape[axis]
    spot = lax.broadcasted_iota(jnp.int32, cells.shape, axis)
    beyond = jnp.where(spot == size - 1, cells_after, pltpu.roll(cells, size - 1, axis))
    face = face_weights(speed * side, speed * (1.0 - side), cells * beyond)
    first = cells[:1, :] if axis == 0 else cells[:, :1]
    entry = face_weights(speed_before * side_before, speed_before * (1.0 - side_before), cells_before * first)
    result = {}
    for s in range(-3, 4):
        value = 0.0
        if s + 1 in face:
            value = value + jnp.where(spot == 0, entry[s + 1], pltpu.roll(face[s + 1], 1, axis))
        if s in face:
            value = value - face[s]
        result[s] = cells * value
    return result


def interior_kernel(
    field, mean, east, north, flag_east, flag_north, mask, side_before, side_after, before, after,
    out, mean_next, l3, l2, l1, h1, h2, h3, *coefs,
):
    coefs_x, coefs_y, centre, vertical = coefs[:6], coefs[6:12], coefs[12], coefs[13]
    group, levels, size_x, size_y = field.shape
    modes = group * pl.num_programs(0)
    f0 = pl.program_id(0) * group
    lane = lax.broadcasted_iota(jnp.int32, (size_x, LANES), 1)
    tiles = size_y // LANES
    shifts = (-3, -2, -1, 1, 2, 3)

    def columns_around(k, f, read):
        left = pltpu.roll(before[k], LANES - HALO - HALO * f, 1)
        right = pltpu.roll(after[k], LANES - HALO * f, 1)
        return [left] + [read(slice(t * LANES, (t + 1) * LANES)) for t in range(tiles)] + [right]

    def moved(row, t, s):
        if s < 0:
            mixed = jnp.where(lane >= LANES + s, row[t], row[t + 1])
        else:
            mixed = jnp.where(lane < s, row[t + 2], row[t + 1])
        return pltpu.roll(mixed, (-s) % LANES, 1)

    @pl.when(pl.program_id(0) == 0)
    def _():
        spot = lax.broadcasted_iota(jnp.int32, (size_x, size_y), 0)
        at = HALO * field.shape[0] * pl.num_programs(0)
        column = lax.broadcasted_iota(jnp.int32, (size_x, LANES), 1)

        def picked(ref, k, offset):
            return jnp.sum(jnp.where(column == at + offset, ref[k], 0.0), axis=1, keepdims=True)

        def prepare(k, carry):
            wet = mask[k].astype(jnp.float32)
            low = [side_before[j, pl.ds(k, 1), :] for j in range(HALO + 3)]
            high = [side_after[j, pl.ds(k, 1), :] for j in range(HALO + 1)]
            dx = stencil(
                east[k], flag_east[k].astype(jnp.float32), wet, low[HALO + 1], low[HALO + 2], low[HALO], high[HALO], 0
            )
            dy = stencil(
                north[k],
                flag_north[k].astype(jnp.float32),
                wet,
                picked(before, k, HALO + 1),
                picked(before, k, HALO + 2),
                picked(before, k, HALO),
                picked(after, k, HALO),
                1,
            )
            middle = dx[0] + dy[0] - 2.0 * vert_diff * wet
            upright = vert_diff * wet
            centre[k] = middle
            vertical[k] = upright
            c = mean[k]
            around = mean[jnp.minimum(k + 1, levels - 1)] + mean[jnp.maximum(k - 1, 0)]
            total = middle * c + upright * around
            row = columns_around(k, modes, lambda cut: mean[k, :, cut])
            for i, s in enumerate(shifts):
                inside = (spot + s >= 0) & (spot + s < size_x)
                coefs_x[i][k] = jnp.where(inside, dx[s], 0.0)
                outside = jnp.where(inside, 0.0, dx[s])
                if s < 0:
                    (l3, l2, l1)[i][k] = outside[:SUB]
                else:
                    (h1, h2, h3)[i - 3][k] = outside[size_x - SUB :]
                coefs_y[i][k] = dy[s]
                shifted = pltpu.roll(c, (-s) % size_x, 0)
                for j in range(abs(s)):
                    if s < 0:
                        shifted = jnp.where(spot == j, low[HALO + s + j], shifted)
                    else:
                        shifted = jnp.where(spot == size_x - s + j, high[j], shifted)
                total += dx[s] * shifted
                total += dy[s] * jnp.concatenate([moved(row, t, s) for t in range(tiles)], axis=1)
            mean_next[k] = c + time_step * total
            return carry

        lax.fori_loop(0, levels, prepare, 0)

    def level(k, carry):
        above = jnp.minimum(k + 1, levels - 1)
        below = jnp.maximum(k - 1, 0)
        for g in range(group):
            row = columns_around(k, f0 + g, lambda cut: field[g, k, :, cut])
            for t in range(tiles):
                cut = slice(t * LANES, (t + 1) * LANES)
                c = row[t + 1]
                total = centre[k, :, cut] * c + vertical[k, :, cut] * (field[g, above, :, cut] + field[g, below, :, cut])
                for i, s in enumerate(shifts):
                    total += coefs_x[i][k, :, cut] * pltpu.roll(c, (-s) % size_x, 0)
                    total += coefs_y[i][k, :, cut] * moved(row, t, s)
                out[g, k, :, cut] = total
        return carry

    lax.fori_loop(0, levels, level, 0, unroll=2)


def gram_kernel(
    nx, ny, modes, partial, low, high, l3, l2, l1, h1, h2, h3, tend, gram,
    low_rows, high_rows, total, mine, middle, along_y, along_x, send_y, recv_y, send_x, recv_x,
):
    z = pl.program_id(0)
    gx, gy = lax.axis_index("gx"), lax.axis_index("gy")
    barrier = pltpu.get_barrier_semaphore()
    count, levels, size_x, size_y = modes.shape

    rows = low.shape[1]
    wide = 2 * count * SUB

    def next_y(k):
        return lax.rem(gy + k, ny)

    def next_x(k):
        return lax.rem(gx + k, nx)

    def copy_y(k, slot):
        return pltpu.make_async_remote_copy(
            src_ref=mine,
            dst_ref=along_y.at[slot],
            send_sem=send_y.at[k],
            recv_sem=recv_y.at[slot],
            device_id=(gx, next_y(k)),
            device_id_type=MESH,
        )

    def copy_x(k, slot):
        return pltpu.make_async_remote_copy(
            src_ref=middle,
            dst_ref=along_x.at[slot],
            send_sem=send_x.at[k],
            recv_sem=recv_x.at[slot],
            device_id=(next_x(k), gy),
            device_id_type=MESH,
        )

    @pl.when(z == 0)
    def _():
        for k in range(1, ny):
            pl.semaphore_signal(barrier, inc=1, device_id=(gx, next_y(k)), device_id_type=MESH)
        for k in range(1, nx):
            pl.semaphore_signal(barrier, inc=1, device_id=(next_x(k), gy), device_id_type=MESH)
        low_rows[...] = jnp.zeros_like(low_rows)
        high_rows[...] = jnp.zeros_like(high_rows)
        total[...] = jnp.zeros_like(total)

    for k in range(levels):
        low_rows[k, SUB : SUB + rows, :] = low[k]
        high_rows[k, SUB : SUB + rows, :] = high[k]
        for f in range(count):
            at = SUB + HALO * f
            if size_x > 2 * SUB:
                tend[f, k] = partial[f, k]
            tend[f, k, :SUB, :] = partial[f, k, :SUB, :] + (
                l3[k] * low_rows[k, at : at + SUB, :]
                + l2[k] * low_rows[k, at + 1 : at + 1 + SUB, :]
                + l1[k] * low_rows[k, at + 2 : at + 2 + SUB, :]
            )
            base = tend if size_x == SUB else partial
            tend[f, k, size_x - SUB :, :] = base[f, k, size_x - SUB :, :] + (
                h1[k] * high_rows[k, at - 7 : at - 7 + SUB, :]
                + h2[k] * high_rows[k, at - 6 : at - 6 + SUB, :]
                + h3[k] * high_rows[k, at - 5 : at - 5 + SUB, :]
            )
    contract = (((1,), (1,)), ((), ()))
    for part in range(size_x // SUB):
        cut = slice(part * SUB, (part + 1) * SUB)
        both = jnp.concatenate(
            [
                jnp.concatenate([ref[:, k, cut, :].reshape(count * SUB, size_y) for k in range(levels)], axis=1)
                for ref in (modes, tend)
            ],
            axis=0,
        )
        coarse = both.astype(jnp.bfloat16)
        fine = (both - coarse.astype(jnp.float32)).astype(jnp.bfloat16)
        total[...] += lax.dot_general(
            jnp.concatenate([coarse, fine], axis=0), coarse, contract, preferred_element_type=jnp.float32
        )

    @pl.when(z == pl.num_programs(0) - 1)
    def _():
        row = lax.broadcasted_iota(jnp.int32, (wide, wide), 0)
        col = lax.broadcasted_iota(jnp.int32, (wide, wide), 1)
        kept = (row % SUB) == (col % SUB)
        cross = total[wide:, :]
        summed = jnp.where(kept, total[:wide, :] + cross + cross.T, 0.0)
        pick = (
            lax.broadcasted_iota(jnp.int32, (2 * count, wide), 1) // SUB
            == lax.broadcasted_iota(jnp.int32, (2 * count, wide), 0)
        ).astype(jnp.float32)
        width = gram.shape[1]
        spread = (
            lax.broadcasted_iota(jnp.int32, (wide, width), 0) // SUB
            == lax.broadcasted_iota(jnp.int32, (wide, width), 1) % (2 * count)
        ).astype(jnp.float32)
        half = jnp.dot(pick, summed, precision=HIGHEST, preferred_element_type=jnp.float32)
        full = jnp.dot(half, spread, precision=HIGHEST, preferred_element_type=jnp.float32)
        height = gram.shape[0]
        block = lax.broadcasted_iota(jnp.int32, gram.shape, 1) // (2 * count)
        packed = full[:height]
        for b in range(1, 2 * count // height):
            packed = jnp.where(block == b, full[b * height : (b + 1) * height], packed)
        mine[...] = packed
        along_y[gy] = packed
        pl.semaphore_wait(barrier, nx + ny - 2)
        for k in range(1, ny):
            copy_y(k, gy).start()
        for k in range(1, ny):
            copy_y(k, next_y(k)).wait_recv()
        summed = along_y[0]
        for k in range(1, ny):
            summed = summed + along_y[k]
        middle[...] = summed
        along_x[gx] = summed
        for k in range(1, ny):
            copy_y(k, gy).wait_send()
        for k in range(1, nx):
            copy_x(k, gx).start()
        for k in range(1, nx):
            copy_x(k, next_x(k)).wait_recv()
        summed = along_x[0]
        for k in range(1, nx):
            summed = summed + along_x[k]
        gram[...] = summed
        for k in range(1, nx):
            copy_x(k, gx).wait_send()


def solve(packed, count, cells):
    two = 2 * count
    height, width = packed.shape
    block = lax.broadcasted_iota(jnp.int32, packed.shape, 1) // two
    stacked = jnp.concatenate([jnp.where(block == b, packed, 0.0) for b in range(two // height)], axis=0)
    fold = (
        lax.broadcasted_iota(jnp.int32, (width, two), 0) % two == lax.broadcasted_iota(jnp.int32, (width, two), 1)
    ).astype(jnp.float32)
    total = jnp.dot(stacked, fold, precision=HIGHEST, preferred_element_type=jnp.float32) / cells
    row = lax.broadcasted_iota(jnp.int32, (count, two), 0)
    col = lax.broadcasted_iota(jnp.int32, (count, two), 1)
    contract = (((1,), (1,)), ((), ()))
    update = jnp.where(
        col < count,
        jnp.where(col == row, 1.0, 0.0) - time_step * total[count:, :],
        jnp.where(col == row + count, time_step, 0.0),
    )
    padding = jnp.zeros((count, two), jnp.float32)
    halfway = jnp.dot(update, total, precision=HIGHEST, preferred_element_type=jnp.float32)
    work = lax.dot_general(
        halfway,
        jnp.concatenate([update, padding], axis=0),
        contract,
        precision=HIGHEST,
        preferred_element_type=jnp.float32,
    )
    work = work + jnp.where(col == row + count, 1.0, 0.0)
    for j in range(count):
        column = jnp.broadcast_to(work[:, j : j + 1], (count, two))
        scale = lax.rsqrt(column[j : j + 1, :])
        pivot_row = work[j : j + 1, :] * scale
        work = jnp.where(row > j, work - (column * scale) * pivot_row, jnp.where(row == j, pivot_row, work))
    factor = jnp.where(col >= row, work, 0.0)[:, :count]
    inverse = jnp.where(col >= count, work, 0.0)
    mix = jnp.dot(
        inverse,
        jnp.concatenate([padding, update], axis=0),
        precision=HIGHEST,
        preferred_element_type=jnp.float32,
    )
    return factor, mix


def combine_kernel(cells, packed, modes, tend, out, factor, weights):
    z = pl.program_id(0)
    count, levels, size_x, size_y = modes.shape
    tall, wide = count * SUB, 2 * count * SUB

    @pl.when(z == 0)
    def _():
        factor[...], mix = solve(packed[...], count, cells)
        spread = (
            lax.broadcasted_iota(jnp.int32, (tall, count), 0) // SUB
            == lax.broadcasted_iota(jnp.int32, (tall, count), 1)
        ).astype(jnp.float32)
        along = (
            lax.broadcasted_iota(jnp.int32, (2 * count, wide), 1) // SUB
            == lax.broadcasted_iota(jnp.int32, (2 * count, wide), 0)
        ).astype(jnp.float32)
        whole = jnp.dot(
            jnp.dot(spread, mix, precision=HIGHEST, preferred_element_type=jnp.float32),
            along,
            precision=HIGHEST,
            preferred_element_type=jnp.float32,
        )
        row = lax.broadcasted_iota(jnp.int32, (tall, wide), 0)
        col = lax.broadcasted_iota(jnp.int32, (tall, wide), 1)
        whole = jnp.where((row % SUB) == (col % SUB), whole, 0.0)
        coarse = whole.astype(jnp.bfloat16)
        weights[:tall, :] = coarse
        weights[tall:, :] = (whole - coarse.astype(jnp.float32)).astype(jnp.bfloat16)

    for k in range(levels):
        for part in range(size_x // SUB):
            cut = slice(part * SUB, (part + 1) * SUB)
            both = jnp.concatenate(
                [modes[:, k, cut, :].reshape(count * SUB, size_y), tend[:, k, cut, :].reshape(count * SUB, size_y)],
                axis=0,
            )
            coarse = both.astype(jnp.bfloat16)
            fine = (both - coarse.astype(jnp.float32)).astype(jnp.bfloat16)
            main = jnp.dot(weights[...], coarse, preferred_element_type=jnp.float32)
            result = main[:tall] + (
                main[tall:] + jnp.dot(weights[:tall, :], fine, preferred_element_type=jnp.float32)
            )
            out[:, k, cut, :] = result.reshape(count, SUB, size_y)


def divisor(size, most):
    return max(d for d in range(1, most + 1) if size % d == 0)


def section(mean_field, mode_fields, velocity_east, velocity_north, flag_east, flag_north, ocean_mask):
    count, levels, size_x, size_y = mode_fields.shape
    nx, ny = lax.axis_size("gx"), lax.axis_size("gy")
    f32 = jnp.float32

    def up(value, axis):
        return lax.ppermute(value, axis, [(i, i + 1) for i in range(lax.axis_size(axis) - 1)])

    def down(value, axis):
        return lax.ppermute(value, axis, [(i + 1, i) for i in range(lax.axis_size(axis) - 1)])

    step = divisor(levels, 4)
    modes_level = pl.BlockSpec((count, step, size_x, size_y), lambda z: (0, z, 0, 0))
    layers = pl.BlockSpec((step, HALO * count, size_y), lambda z: (z, 0, 0))
    whole_plane = pl.BlockSpec((levels, size_x, size_y), lambda z: (0, 0, 0))
    side_rows = (HALO + 3, HALO + 1)
    x_last, x_first, aux_last, aux_first = pl.pallas_call(
        layers_kernel,
        grid=(levels // step,),
        in_specs=[modes_level] + [whole_plane] * 4,
        out_specs=[layers, layers] + [pl.BlockSpec((n, levels, size_y), lambda z: (0, 0, 0)) for n in side_rows],
        out_shape=[jax.ShapeDtypeStruct((levels, HALO * count, size_y), f32)] * 2
        + [jax.ShapeDtypeStruct((n, levels, size_y), f32) for n in side_rows],
    )(mode_fields, mean_field, velocity_east, flag_east, ocean_mask)
    aux_before = up(aux_last, "gx")
    aux_after = down(aux_first, "gx")
    x_before = up(x_last, "gx")
    x_after = down(x_first, "gx")

    half = SUB if levels % SUB == 0 else levels
    plane = pl.BlockSpec((half, size_x, size_y), lambda z: (z, 0, 0))
    columns = pl.BlockSpec((half, size_x, LANES), lambda z: (z, 0, 0))
    y_last, y_first = pl.pallas_call(
        columns_kernel,
        grid=(levels // half,),
        in_specs=[pl.BlockSpec(memory_space=pl.ANY)]
        + [pl.BlockSpec((count, half, size_x, size_y), lambda z: (0, z, 0, 0))]
        + [plane] * 4,
        out_specs=[columns, columns],
        out_shape=[jax.ShapeDtypeStruct((levels, size_x, LANES), f32)] * 2,
    )(x_last, mode_fields, mean_field, velocity_north, flag_north, ocean_mask)
    y_before, y_after = up(y_last, "gy"), down(y_first, "gy")

    group = divisor(count, 2)
    one_field = pl.BlockSpec((group, levels, size_x, size_y), lambda f: (f, 0, 0, 0))
    plane_whole = pl.BlockSpec((levels, size_x, size_y), lambda f: (0, 0, 0))
    halo_whole = pl.BlockSpec((levels, size_x, LANES), lambda f: (0, 0, 0))
    cost = pl.CostEstimate(flops=60 * mode_fields.size, bytes_accessed=12 * mode_fields.size, transcendentals=0)
    partial, mean_next, *outer = pl.pallas_call(
        interior_kernel,
        grid=(count // group,),
        in_specs=[one_field]
        + [plane_whole] * 6
        + [pl.BlockSpec((n, levels, size_y), lambda f: (0, 0, 0)) for n in side_rows]
        + [halo_whole] * 2,
        out_specs=[one_field, plane_whole] + [pl.BlockSpec((levels, SUB, size_y), lambda f: (0, 0, 0))] * 6,
        out_shape=[jax.ShapeDtypeStruct(mode_fields.shape, f32), jax.ShapeDtypeStruct(mean_field.shape, f32)]
        + [jax.ShapeDtypeStruct((levels, SUB, size_y), f32)] * 6,
        scratch_shapes=[pltpu.VMEM((levels, size_x, size_y), f32)] * 14,
        cost_estimate=cost,
    )(
        mode_fields, mean_field, velocity_east, velocity_north, flag_east, flag_north, ocean_mask,
        aux_before, aux_after, y_before, y_after,
    )

    edge = pl.BlockSpec((step, SUB, size_y), lambda z: (z, 0, 0))
    wide = 2 * count * SUB
    packed = (4 * count * count // LANES, LANES)
    tend, gram = pl.pallas_call(
        functools.partial(gram_kernel, nx, ny),
        grid=(levels // step,),
        in_specs=[modes_level, modes_level, layers, layers] + [edge] * 6,
        out_specs=[modes_level, pl.BlockSpec(packed, lambda z: (0, 0))],
        out_shape=[jax.ShapeDtypeStruct(mode_fields.shape, f32), jax.ShapeDtypeStruct(packed, f32)],
        scratch_shapes=[pltpu.VMEM((step, HALO * count + 2 * SUB, size_y), f32)] * 2
        + [
            pltpu.VMEM((2 * wide, wide), f32),
            pltpu.VMEM(packed, f32),
            pltpu.VMEM(packed, f32),
            pltpu.VMEM((ny,) + packed, f32),
            pltpu.VMEM((nx,) + packed, f32),
            pltpu.SemaphoreType.DMA((ny,)),
            pltpu.SemaphoreType.DMA((ny,)),
            pltpu.SemaphoreType.DMA((nx,)),
            pltpu.SemaphoreType.DMA((nx,)),
        ],
        compiler_params=pltpu.CompilerParams(collective_id=0, has_side_effects=True),
    )(mode_fields, partial, x_before, x_after, *outer)

    cell_count = float(levels * size_x * size_y * nx * ny)
    modes_next, factor = pl.pallas_call(
        functools.partial(combine_kernel, cell_count),
        grid=(levels // step,),
        in_specs=[pl.BlockSpec(packed, lambda z: (0, 0)), modes_level, modes_level],
        out_specs=[modes_level, pl.BlockSpec((count, count), lambda z: (0, 0))],
        out_shape=[jax.ShapeDtypeStruct(mode_fields.shape, f32), jax.ShapeDtypeStruct((count, count), f32)],
        scratch_shapes=[pltpu.VMEM((wide, wide), jnp.bfloat16)],
    )(gram, mode_fields, tend)
    return (mean_next, modes_next, factor)


def solution(mesh):
    grid = P(None, "gx", "gy")
    return jax.shard_map(
        section,
        mesh=mesh,
        in_specs=(grid, P(None, None, "gx", "gy"), grid, grid, grid, grid, grid),
        out_specs=(grid, P(None, None, "gx", "gy"), P()),
        check_vma=False,
    )
```

```python
import functools

import jax
import jax.numpy as jnp
from jax import lax
from jax.experimental import pallas as pl
from jax.experimental.pallas import tpu as pltpu
from jax.sharding import PartitionSpec as P


time_step = 0.1
horiz_diff = 0.05
vert_diff = 0.2
HALO = 3
LANES = 128
SUB = 8
HIGHEST = lax.Precision.HIGHEST
MESH = pl.DeviceIdType.MESH


def layers_kernel(modes, mean, east, flag, mask, x_last, x_first, aux_last, aux_first):
    count, levels, size_x, _ = modes.shape

    @pl.when(pl.program_id(0) == 0)
    def _():
        for j in range(HALO):
            aux_last[j] = mean[:, size_x - HALO + j, :]
            aux_first[j] = mean[:, j, :]
        aux_last[HALO] = mask[:, size_x - 1, :].astype(jnp.float32)
        aux_first[HALO] = mask[:, 0, :].astype(jnp.float32)
        aux_last[HALO + 1] = east[:, size_x - 1, :]
        aux_last[HALO + 2] = flag[:, size_x - 1, :].astype(jnp.float32)

    for k in range(levels):
        for f in range(count):
            x_last[k, HALO * f : HALO * (f + 1), :] = modes[f, k, size_x - HALO :, :]
            x_first[k, HALO * f : HALO * (f + 1), :] = modes[f, k, :HALO, :]


def columns_kernel(after_layers, modes, mean, north, flag_north, mask, y_last, y_first):
    count, levels, size_x, size_y = modes.shape
    lane = lax.broadcasted_iota(jnp.int32, (size_x, LANES), 1)

    def put(packed, tile, source_lane, target_lane, width):
        moved = pltpu.roll(tile, (target_lane - source_lane) % LANES, 1)
        return jnp.where((lane >= target_lane) & (lane < target_lane + width), moved, packed)

    for k in range(levels):
        mask_value = mask[k].astype(jnp.float32)
        last = jnp.zeros((size_x, LANES), jnp.float32)
        first = jnp.zeros((size_x, LANES), jnp.float32)
        for f in range(count):
            last = put(last, modes[f, k, :, size_y - LANES :], LANES - HALO, HALO * f, HALO)
            first = put(first, modes[f, k, :, :LANES], 0, HALO * f, HALO)
        base = HALO * count
        last = put(last, mean[k, :, size_y - LANES :], LANES - HALO, base, HALO)
        first = put(first, mean[k, :, :LANES], 0, base, HALO)
        base += HALO
        last = put(last, mask_value[:, size_y - LANES :], LANES - 1, base, 1)
        first = put(first, mask_value[:, :LANES], 0, base, 1)
        last = put(last, north[k, :, size_y - LANES :], LANES - 1, base + 1, 1)
        last = put(last, flag_north[k, :, size_y - LANES :].astype(jnp.float32), LANES - 1, base + 2, 1)
        y_last[k] = last
        y_first[k] = first


def face_weights(pos, neg, openness):
    return {
        -2: openness * (2.0 * pos) / 60.0,
        -1: openness * (-13.0 * pos - 3.0 * neg) / 60.0,
        0: openness * ((47.0 * pos + 27.0 * neg) / 60.0 + horiz_diff),
        1: openness * ((27.0 * pos + 47.0 * neg) / 60.0 - horiz_diff),
        2: openness * (-3.0 * pos - 13.0 * neg) / 60.0,
        3: openness * (2.0 * neg) / 60.0,
    }


def stencil(speed, side, cells, speed_before, side_before, cells_before, cells_after, axis):
    size = cells.shape[axis]
    spot = lax.broadcasted_iota(jnp.int32, cells.shape, axis)
    beyond = jnp.where(spot == size - 1, cells_after, pltpu.roll(cells, size - 1, axis))
    face = face_weights(speed * side, speed * (1.0 - side), cells * beyond)
    first = cells[:1, :] if axis == 0 else cells[:, :1]
    entry = face_weights(speed_before * side_before, speed_before * (1.0 - side_before), cells_before * first)
    result = {}
    for s in range(-3, 4):
        value = 0.0
        if s + 1 in face:
            value = value + jnp.where(spot == 0, entry[s + 1], pltpu.roll(face[s + 1], 1, axis))
        if s in face:
            value = value - face[s]
        result[s] = cells * value
    return result


def interior_kernel(
    field, mean, east, north, flag_east, flag_north, mask, side_before, side_after, before, after,
    out, mean_next, l3, l2, l1, h1, h2, h3, *coefs,
):
    coefs_x, coefs_y, centre, vertical = coefs[:6], coefs[6:12], coefs[12], coefs[13]
    group, levels, size_x, size_y = field.shape
    modes = group * pl.num_programs(0)
    f0 = pl.program_id(0) * group
    lane = lax.broadcasted_iota(jnp.int32, (size_x, LANES), 1)
    tiles = size_y // LANES
    shifts = (-3, -2, -1, 1, 2, 3)

    def columns_around(k, f, read):
        left = pltpu.roll(before[k], LANES - HALO - HALO * f, 1)
        right = pltpu.roll(after[k], LANES - HALO * f, 1)
        return [left] + [read(slice(t * LANES, (t + 1) * LANES)) for t in range(tiles)] + [right]

    def moved(row, t, s):
        if s < 0:
            mixed = jnp.where(lane >= LANES + s, row[t], row[t + 1])
        else:
            mixed = jnp.where(lane < s, row[t + 2], row[t + 1])
        return pltpu.roll(mixed, (-s) % LANES, 1)

    @pl.when(pl.program_id(0) == 0)
    def _():
        spot = lax.broadcasted_iota(jnp.int32, (size_x, size_y), 0)
        at = HALO * field.shape[0] * pl.num_programs(0)
        column = lax.broadcasted_iota(jnp.int32, (size_x, LANES), 1)

        def picked(ref, k, offset):
            return jnp.sum(jnp.where(column == at + offset, ref[k], 0.0), axis=1, keepdims=True)

        def prepare(k, carry):
            wet = mask[k].astype(jnp.float32)
            low = [side_before[j, pl.ds(k, 1), :] for j in range(HALO + 3)]
            high = [side_after[j, pl.ds(k, 1), :] for j in range(HALO + 1)]
            dx = stencil(
                east[k], flag_east[k].astype(jnp.float32), wet, low[HALO + 1], low[HALO + 2], low[HALO], high[HALO], 0
            )
            dy = stencil(
                north[k],
                flag_north[k].astype(jnp.float32),
                wet,
                picked(before, k, HALO + 1),
                picked(before, k, HALO + 2),
                picked(before, k, HALO),
                picked(after, k, HALO),
                1,
            )
            middle = dx[0] + dy[0] - 2.0 * vert_diff * wet
            upright = vert_diff * wet
            centre[k] = middle
            vertical[k] = upright
            c = mean[k]
            around = mean[jnp.minimum(k + 1, levels - 1)] + mean[jnp.maximum(k - 1, 0)]
            total = middle * c + upright * around
            row = columns_around(k, modes, lambda cut: mean[k, :, cut])
            for i, s in enumerate(shifts):
                inside = (spot + s >= 0) & (spot + s < size_x)
                coefs_x[i][k] = jnp.where(inside, dx[s], 0.0)
                outside = jnp.where(inside, 0.0, dx[s])
                if s < 0:
                    (l3, l2, l1)[i][k] = outside[:SUB]
                else:
                    (h1, h2, h3)[i - 3][k] = outside[size_x - SUB :]
                coefs_y[i][k] = dy[s]
                shifted = pltpu.roll(c, (-s) % size_x, 0)
                for j in range(abs(s)):
                    if s < 0:
                        shifted = jnp.where(spot == j, low[HALO + s + j], shifted)
                    else:
                        shifted = jnp.where(spot == size_x - s + j, high[j], shifted)
                total += dx[s] * shifted
                total += dy[s] * jnp.concatenate([moved(row, t, s) for t in range(tiles)], axis=1)
            mean_next[k] = c + time_step * total
            return carry

        lax.fori_loop(0, levels, prepare, 0)

    def level(k, carry):
        above = jnp.minimum(k + 1, levels - 1)
        below = jnp.maximum(k - 1, 0)
        for g in range(group):
            row = columns_around(k, f0 + g, lambda cut: field[g, k, :, cut])
            for t in range(tiles):
                cut = slice(t * LANES, (t + 1) * LANES)
                c = row[t + 1]
                total = centre[k, :, cut] * c + vertical[k, :, cut] * (field[g, above, :, cut] + field[g, below, :, cut])
                for i, s in enumerate(shifts):
                    total += coefs_x[i][k, :, cut] * pltpu.roll(c, (-s) % size_x, 0)
                    total += coefs_y[i][k, :, cut] * moved(row, t, s)
                out[g, k, :, cut] = total
        return carry

    lax.fori_loop(0, levels, level, 0, unroll=2)


def gram_kernel(
    nx, ny, modes, partial, low, high, l3, l2, l1, h1, h2, h3, tend, gram,
    low_rows, high_rows, total, mine, middle, along_y, along_x, send_y, recv_y, send_x, recv_x,
):
    z = pl.program_id(0)
    gx, gy = lax.axis_index("gx"), lax.axis_index("gy")
    barrier = pltpu.get_barrier_semaphore()
    count, levels, size_x, size_y = modes.shape

    rows = low.shape[1]
    wide = 2 * count * SUB

    def next_y(k):
        return lax.rem(gy + k, ny)

    def next_x(k):
        return lax.rem(gx + k, nx)

    def copy_y(k, slot):
        return pltpu.make_async_remote_copy(
            src_ref=mine,
            dst_ref=along_y.at[slot],
            send_sem=send_y.at[k],
            recv_sem=recv_y.at[slot],
            device_id=(gx, next_y(k)),
            device_id_type=MESH,
        )

    def copy_x(k, slot):
        return pltpu.make_async_remote_copy(
            src_ref=middle,
            dst_ref=along_x.at[slot],
            send_sem=send_x.at[k],
            recv_sem=recv_x.at[slot],
            device_id=(next_x(k), gy),
            device_id_type=MESH,
        )

    @pl.when(z == 0)
    def _():
        for k in range(1, ny):
            pl.semaphore_signal(barrier, inc=1, device_id=(gx, next_y(k)), device_id_type=MESH)
        for k in range(1, nx):
            pl.semaphore_signal(barrier, inc=1, device_id=(next_x(k), gy), device_id_type=MESH)
        low_rows[...] = jnp.zeros_like(low_rows)
        high_rows[...] = jnp.zeros_like(high_rows)
        total[...] = jnp.zeros_like(total)

    for k in range(levels):
        low_rows[k, SUB : SUB + rows, :] = low[k]
        high_rows[k, SUB : SUB + rows, :] = high[k]
        for f in range(count):
            at = SUB + HALO * f
            if size_x > 2 * SUB:
                tend[f, k] = partial[f, k]
            tend[f, k, :SUB, :] = partial[f, k, :SUB, :] + (
                l3[k] * low_rows[k, at : at + SUB, :]
                + l2[k] * low_rows[k, at + 1 : at + 1 + SUB, :]
                + l1[k] * low_rows[k, at + 2 : at + 2 + SUB, :]
            )
            base = tend if size_x == SUB else partial
            tend[f, k, size_x - SUB :, :] = base[f, k, size_x - SUB :, :] + (
                h1[k] * high_rows[k, at - 7 : at - 7 + SUB, :]
                + h2[k] * high_rows[k, at - 6 : at - 6 + SUB, :]
                + h3[k] * high_rows[k, at - 5 : at - 5 + SUB, :]
            )
    contract = (((1,), (1,)), ((), ()))
    for part in range(size_x // SUB):
        cut = slice(part * SUB, (part + 1) * SUB)
        both = jnp.concatenate(
            [
                jnp.concatenate([ref[:, k, cut, :].reshape(count * SUB, size_y) for k in range(levels)], axis=1)
                for ref in (modes, tend)
            ],
            axis=0,
        )
        coarse = both.astype(jnp.bfloat16)
        fine = (both - coarse.astype(jnp.float32)).astype(jnp.bfloat16)
        total[...] += lax.dot_general(
            jnp.concatenate([coarse, fine], axis=0), coarse, contract, preferred_element_type=jnp.float32
        )

    @pl.when(z == pl.num_programs(0) - 1)
    def _():
        row = lax.broadcasted_iota(jnp.int32, (wide, wide), 0)
        col = lax.broadcasted_iota(jnp.int32, (wide, wide), 1)
        kept = (row % SUB) == (col % SUB)
        cross = total[wide:, :]
        summed = jnp.where(kept, total[:wide, :] + cross + cross.T, 0.0)
        pick = (
            lax.broadcasted_iota(jnp.int32, (2 * count, wide), 1) // SUB
            == lax.broadcasted_iota(jnp.int32, (2 * count, wide), 0)
        ).astype(jnp.float32)
        width = gram.shape[1]
        spread = (
            lax.broadcasted_iota(jnp.int32, (wide, width), 0) // SUB
            == lax.broadcasted_iota(jnp.int32, (wide, width), 1) % (2 * count)
        ).astype(jnp.float32)
        half = jnp.dot(pick, summed, precision=HIGHEST, preferred_element_type=jnp.float32)
        full = jnp.dot(half, spread, precision=HIGHEST, preferred_element_type=jnp.float32)
        height = gram.shape[0]
        block = lax.broadcasted_iota(jnp.int32, gram.shape, 1) // (2 * count)
        packed = full[:height]
        for b in range(1, 2 * count // height):
            packed = jnp.where(block == b, full[b * height : (b + 1) * height], packed)
        mine[...] = packed
        along_y[gy] = packed
        pl.semaphore_wait(barrier, nx + ny - 2)
        for k in range(1, ny):
            copy_y(k, gy).start()
        for k in range(1, ny):
            copy_y(k, next_y(k)).wait_recv()
        summed = along_y[0]
        for k in range(1, ny):
            summed = summed + along_y[k]
        middle[...] = summed
        along_x[gx] = summed
        for k in range(1, ny):
            copy_y(k, gy).wait_send()
        for k in range(1, nx):
            copy_x(k, gx).start()
        for k in range(1, nx):
            copy_x(k, next_x(k)).wait_recv()
        summed = along_x[0]
        for k in range(1, nx):
            summed = summed + along_x[k]
        gram[...] = summed
        for k in range(1, nx):
            copy_x(k, gx).wait_send()


def solve(packed, count, cells):
    two = 2 * count
    height, width = packed.shape
    block = lax.broadcasted_iota(jnp.int32, packed.shape, 1) // two
    stacked = jnp.concatenate([jnp.where(block == b, packed, 0.0) for b in range(two // height)], axis=0)
    fold = (
        lax.broadcasted_iota(jnp.int32, (width, two), 0) % two == lax.broadcasted_iota(jnp.int32, (width, two), 1)
    ).astype(jnp.float32)
    total = jnp.dot(stacked, fold, precision=HIGHEST, preferred_element_type=jnp.float32) / cells
    row = lax.broadcasted_iota(jnp.int32, (count, two), 0)
    col = lax.broadcasted_iota(jnp.int32, (count, two), 1)
    contract = (((1,), (1,)), ((), ()))
    update = jnp.where(
        col < count,
        jnp.where(col == row, 1.0, 0.0) - time_step * total[count:, :],
        jnp.where(col == row + count, time_step, 0.0),
    )
    padding = jnp.zeros((count, two), jnp.float32)
    halfway = jnp.dot(update, total, precision=HIGHEST, preferred_element_type=jnp.float32)
    work = lax.dot_general(
        halfway,
        jnp.concatenate([update, padding], axis=0),
        contract,
        precision=HIGHEST,
        preferred_element_type=jnp.float32,
    )
    work = work + jnp.where(col == row + count, 1.0, 0.0)
    for j in range(count):
        column = jnp.broadcast_to(work[:, j : j + 1], (count, two))
        scale = lax.rsqrt(column[j : j + 1, :])
        pivot_row = work[j : j + 1, :] * scale
        work = jnp.where(row > j, work - (column * scale) * pivot_row, jnp.where(row == j, pivot_row, work))
    factor = jnp.where(col >= row, work, 0.0)[:, :count]
    inverse = jnp.where(col >= count, work, 0.0)
    mix = jnp.dot(
        inverse,
        jnp.concatenate([padding, update], axis=0),
        precision=HIGHEST,
        preferred_element_type=jnp.float32,
    )
    return factor, mix


def combine_kernel(cells, packed, modes, tend, out, factor, weights):
    z = pl.program_id(0)
    count, levels, size_x, size_y = modes.shape
    tall, wide = count * SUB, 2 * count * SUB

    @pl.when(z == 0)
    def _():
        factor[...], mix = solve(packed[...], count, cells)
        spread = (
            lax.broadcasted_iota(jnp.int32, (tall, count), 0) // SUB
            == lax.broadcasted_iota(jnp.int32, (tall, count), 1)
        ).astype(jnp.bfloat16)
        along = (
            lax.broadcasted_iota(jnp.int32, (2 * count, wide), 1) // SUB
            == lax.broadcasted_iota(jnp.int32, (2 * count, wide), 0)
        ).astype(jnp.bfloat16)
        row = lax.broadcasted_iota(jnp.int32, (tall, wide), 0)
        col = lax.broadcasted_iota(jnp.int32, (tall, wide), 1)
        kept = (row % SUB) == (col % SUB)
        coarse = mix.astype(jnp.bfloat16)
        fine = (mix - coarse.astype(jnp.float32)).astype(jnp.bfloat16)
        for place, value in ((0, coarse), (tall, fine)):
            taller = jnp.dot(spread, value, preferred_element_type=jnp.float32).astype(jnp.bfloat16)
            whole = jnp.dot(taller, along, preferred_element_type=jnp.float32)
            weights[place : place + tall, :] = jnp.where(kept, whole, 0.0).astype(jnp.bfloat16)

    for k in range(levels):
        for part in range(size_x // SUB):
            cut = slice(part * SUB, (part + 1) * SUB)
            both = jnp.concatenate(
                [modes[:, k, cut, :].reshape(count * SUB, size_y), tend[:, k, cut, :].reshape(count * SUB, size_y)],
                axis=0,
            )
            coarse = both.astype(jnp.bfloat16)
            fine = (both - coarse.astype(jnp.float32)).astype(jnp.bfloat16)
            main = jnp.dot(weights[...], coarse, preferred_element_type=jnp.float32)
            result = main[:tall] + (
                main[tall:] + jnp.dot(weights[:tall, :], fine, preferred_element_type=jnp.float32)
            )
            out[:, k, cut, :] = result.reshape(count, SUB, size_y)


def divisor(size, most):
    return max(d for d in range(1, most + 1) if size % d == 0)


def section(mean_field, mode_fields, velocity_east, velocity_north, flag_east, flag_north, ocean_mask):
    count, levels, size_x, size_y = mode_fields.shape
    nx, ny = lax.axis_size("gx"), lax.axis_size("gy")
    f32 = jnp.float32

    def up(value, axis):
        return lax.ppermute(value, axis, [(i, i + 1) for i in range(lax.axis_size(axis) - 1)])

    def down(value, axis):
        return lax.ppermute(value, axis, [(i + 1, i) for i in range(lax.axis_size(axis) - 1)])

    step = divisor(levels, 4)
    modes_level = pl.BlockSpec((count, step, size_x, size_y), lambda z: (0, z, 0, 0))
    layers = pl.BlockSpec((step, HALO * count, size_y), lambda z: (z, 0, 0))
    whole_plane = pl.BlockSpec((levels, size_x, size_y), lambda z: (0, 0, 0))
    side_rows = (HALO + 3, HALO + 1)
    x_last, x_first, aux_last, aux_first = pl.pallas_call(
        layers_kernel,
        grid=(levels // step,),
        in_specs=[modes_level] + [whole_plane] * 4,
        out_specs=[layers, layers] + [pl.BlockSpec((n, levels, size_y), lambda z: (0, 0, 0)) for n in side_rows],
        out_shape=[jax.ShapeDtypeStruct((levels, HALO * count, size_y), f32)] * 2
        + [jax.ShapeDtypeStruct((n, levels, size_y), f32) for n in side_rows],
    )(mode_fields, mean_field, velocity_east, flag_east, ocean_mask)
    aux_before = up(aux_last, "gx")
    aux_after = down(aux_first, "gx")
    x_before = up(x_last, "gx")
    x_after = down(x_first, "gx")

    half = SUB if levels % SUB == 0 else levels
    plane = pl.BlockSpec((half, size_x, size_y), lambda z: (z, 0, 0))
    columns = pl.BlockSpec((half, size_x, LANES), lambda z: (z, 0, 0))
    y_last, y_first = pl.pallas_call(
        columns_kernel,
        grid=(levels // half,),
        in_specs=[pl.BlockSpec(memory_space=pl.ANY)]
        + [pl.BlockSpec((count, half, size_x, size_y), lambda z: (0, z, 0, 0))]
        + [plane] * 4,
        out_specs=[columns, columns],
        out_shape=[jax.ShapeDtypeStruct((levels, size_x, LANES), f32)] * 2,
    )(x_last, mode_fields, mean_field, velocity_north, flag_north, ocean_mask)
    y_before, y_after = up(y_last, "gy"), down(y_first, "gy")

    group = divisor(count, 2)
    one_field = pl.BlockSpec((group, levels, size_x, size_y), lambda f: (f, 0, 0, 0))
    plane_whole = pl.BlockSpec((levels, size_x, size_y), lambda f: (0, 0, 0))
    halo_whole = pl.BlockSpec((levels, size_x, LANES), lambda f: (0, 0, 0))
    cost = pl.CostEstimate(flops=60 * mode_fields.size, bytes_accessed=12 * mode_fields.size, transcendentals=0)
    partial, mean_next, *outer = pl.pallas_call(
        interior_kernel,
        grid=(count // group,),
        in_specs=[one_field]
        + [plane_whole] * 6
        + [pl.BlockSpec((n, levels, size_y), lambda f: (0, 0, 0)) for n in side_rows]
        + [halo_whole] * 2,
        out_specs=[one_field, plane_whole] + [pl.BlockSpec((levels, SUB, size_y), lambda f: (0, 0, 0))] * 6,
        out_shape=[jax.ShapeDtypeStruct(mode_fields.shape, f32), jax.ShapeDtypeStruct(mean_field.shape, f32)]
        + [jax.ShapeDtypeStruct((levels, SUB, size_y), f32)] * 6,
        scratch_shapes=[pltpu.VMEM((levels, size_x, size_y), f32)] * 14,
        cost_estimate=cost,
    )(
        mode_fields, mean_field, velocity_east, velocity_north, flag_east, flag_north, ocean_mask,
        aux_before, aux_after, y_before, y_after,
    )

    edge = pl.BlockSpec((step, SUB, size_y), lambda z: (z, 0, 0))
    wide = 2 * count * SUB
    packed = (4 * count * count // LANES, LANES)
    tend, gram = pl.pallas_call(
        functools.partial(gram_kernel, nx, ny),
        grid=(levels // step,),
        in_specs=[modes_level, modes_level, layers, layers] + [edge] * 6,
        out_specs=[modes_level, pl.BlockSpec(packed, lambda z: (0, 0))],
        out_shape=[jax.ShapeDtypeStruct(mode_fields.shape, f32), jax.ShapeDtypeStruct(packed, f32)],
        scratch_shapes=[pltpu.VMEM((step, HALO * count + 2 * SUB, size_y), f32)] * 2
        + [
            pltpu.VMEM((2 * wide, wide), f32),
            pltpu.VMEM(packed, f32),
            pltpu.VMEM(packed, f32),
            pltpu.VMEM((ny,) + packed, f32),
            pltpu.VMEM((nx,) + packed, f32),
            pltpu.SemaphoreType.DMA((ny,)),
            pltpu.SemaphoreType.DMA((ny,)),
            pltpu.SemaphoreType.DMA((nx,)),
            pltpu.SemaphoreType.DMA((nx,)),
        ],
        compiler_params=pltpu.CompilerParams(collective_id=0, has_side_effects=True),
    )(mode_fields, partial, x_before, x_after, *outer)

    cell_count = float(levels * size_x * size_y * nx * ny)
    small = divisor(levels, 2)
    few_levels = pl.BlockSpec((count, small, size_x, size_y), lambda z: (0, z, 0, 0))
    modes_next, factor = pl.pallas_call(
        functools.partial(combine_kernel, cell_count),
        grid=(levels // small,),
        in_specs=[pl.BlockSpec(packed, lambda z: (0, 0)), few_levels, few_levels],
        out_specs=[few_levels, pl.BlockSpec((count, count), lambda z: (0, 0))],
        out_shape=[jax.ShapeDtypeStruct(mode_fields.shape, f32), jax.ShapeDtypeStruct((count, count), f32)],
        scratch_shapes=[pltpu.VMEM((wide, wide), jnp.bfloat16)],
    )(gram, mode_fields, tend)
    return (mean_next, modes_next, factor)


def solution(mesh):
    grid = P(None, "gx", "gy")
    return jax.shard_map(
        section,
        mesh=mesh,
        in_specs=(grid, P(None, None, "gx", "gy"), grid, grid, grid, grid, grid),
        out_specs=(grid, P(None, None, "gx", "gy"), P()),
        check_vma=False,
    )
```
